32 devices in a mesh: facet: 8 (over y, x, core), pulse: 4 (over z).
Axes of the slice: x: 2, y: 2, z: 4, core: 2. Of those that a mesh axis runs over, the one named last changes fastest.
Arguments:
- facet_positions: float32 [3, 6144], P(None, 'facet'), may hold values from -10 to 10
- reflectivity: float32 [2, 6144], P(None, 'facet'), may hold values from -0.109375 to 0.109375
- block_building: int32 [48], P('facet'), may hold values from 0 to 11, never falling along the last dimension, each value on 1 to 8 neighbouring positions
- visible: int32 [12, 64], P(None, 'pulse'), may hold values from 0 to 1
- platform: float32 [3, 2048], P(None, 'pulse'), may hold values from 30 to 40
Outputs:
- image: float32 [2, 512, 2048], P(None, 'pulse', 'facet')
The draws below stay inside these ranges and needn't reach their ends.
All inputs are finite; a program needn't handle non-finite values.
Results may differ from the reference program's by a relative error of at most 0.017.
Values may be sent and summed in bfloat16 or wider, within the bound.
No kernel may reach another device: no remote copies, remote signals or barrier semaphores. Data moves between devices by JAX's collectives and lax.ppermute only.
A program may use at most 64 MiB of HBM per device.

```python
import math
import jax
import jax.numpy as jnp
import numpy as np
from jax import lax

BLK = 128
PULSES = 2048
PBS = 32
BINS = 512
BIN_LO = 32
BMOST = 8
BIN_HI = 16
FACETS = 6144
FBLK = 48
NBLD = 12
PBLOCKS = 64


def draw_visible(key, part):
    key_first, key_length = jax.random.split(jax.random.fold_in(key, 7))
    first_block = jax.random.randint(key_first, (NBLD, 1), 0, PBLOCKS)
    run_length = jax.random.randint(key_length, (NBLD, 1), max(PBLOCKS // 8, 1), PBLOCKS + 1)
    blocks = jnp.arange(PBLOCKS, dtype=jnp.int32)[None, :]
    return ((blocks - first_block) % PBLOCKS < run_length).astype(jnp.int32)


def levels(own_key, shape, shards, least, top_value):
    loudness, own = 1.0, jax.random.fold_in(own_key, 6)
    for axis_at, blocks in shards:
        steps = jnp.exp(jax.random.uniform(jax.random.fold_in(own, axis_at), (blocks,), jnp.float32, least / len(shards), top_value / len(shards)))
        loudness = loudness * jnp.repeat(steps, shape[axis_at] // blocks).reshape([-1 if axis == axis_at else 1 for axis in range(len(shape))])
    return loudness


def split_up(number_of, total, bound, skew):
    weights = [(1 << 20) // math.isqrt(standing ** skew) + 1 for standing in range(2, number_of + 1)]
    spare, given = total - bound - (number_of - 1), [1] * (number_of - 1)
    while spare > 0:
        movable = [i for i in range(number_of - 1) if given[i] < bound]
        whole, left = sum([weights[i] for i in movable]), spare
        for i in movable:
            addition = min(bound - given[i], max(1, left * weights[i] // whole), spare)
            given[i] = given[i] + addition
            spare = spare - addition
    return np.array([bound] + given)


def uneven_parts(stream_key, number_of, total, most, skew):
    if number_of == 2:
        one = jax.random.randint(stream_key, (), max(1, total - most), min(most, total - 1) + 1)
        return jnp.stack([one, total - one])
    tallies = jnp.asarray(split_up(number_of, total, most, skew), jnp.int32)
    twos = (number_of - 1) // 2
    donor, sink = tallies[1:1 + 2 * twos:2], tallies[2:2 + 2 * twos:2]
    room = jnp.minimum(donor - 1, most - sink)
    passed = jax.random.randint(jax.random.fold_in(stream_key, 1), (twos,), 0, 1 << 20) % (room + 1)
    tallies = tallies.at[1:1 + 2 * twos:2].set(donor - passed).at[2:2 + 2 * twos:2].set(sink + passed)
    return tallies[jax.random.permutation(jax.random.fold_in(stream_key, 2), number_of)]


def bell_draw(stream_key, extent, width, limit, cuts=(), kind=jnp.bfloat16):
    drawn = jax.random.normal(stream_key, extent, jnp.float32) * width
    if len(cuts) > 0:
        drawn = levels(stream_key, extent, cuts, -0.22, 0.18) * drawn
    return jnp.clip(drawn, min=-limit, max=limit).astype(kind)


def setup_inputs(seed: int = 0) -> dict:
    keys = jax.random.split(jax.random.key(seed), 6)
    return {
        "facet_positions": jnp.clip(jax.random.uniform(keys[0], (3, FACETS), jnp.float32, -10.0, 10.0) * levels(keys[0], (3, FACETS), ((1, 8),), -0.4, 0.0), -10.0, 10.0),
        "reflectivity": bell_draw(keys[1], (2, FACETS), (FACETS // 2) ** -0.5, 0.109375, ((1, 8),), jnp.float32),
        "block_building": jnp.searchsorted(jnp.cumsum(uneven_parts(keys[2], NBLD, FBLK, BMOST, 2)), jnp.arange(FBLK), side="right").astype(jnp.int32),
        "visible": draw_visible(jax.random.fold_in(keys[5], 71), 0),
        "platform": jnp.clip(30.0 + 10.0 * jax.random.uniform(keys[4], (3, PULSES), jnp.float32) ** levels(keys[4], (3, PULSES), ((1, 4),), -0.2, 0.2), 30.0, 40.0),
    }


wave_start = 2.0
wave_step = 0.25

def echo_group(positions, weights, antenna):
    offsets = positions[:, None, :] - antenna[:, :, None]
    distance = jnp.sqrt(lax.optimization_barrier(jnp.sum(offsets * offsets, axis=0)))
    upper_index = jnp.arange(BIN_HI, dtype=jnp.float32)
    lower_index = jnp.arange(BIN_LO, dtype=jnp.float32)
    coarse = (wave_start + wave_step * BIN_LO * upper_index)[None, :, None] * distance[:, None, :]
    cosine = jnp.cos(coarse)
    sine_a = jnp.sin(coarse)
    real_a = weights[0][None, None, :] * cosine + weights[1][None, None, :] * sine_a
    imag_a = weights[1][None, None, :] * cosine - weights[0][None, None, :] * sine_a
    table_a = jnp.concatenate([real_a, imag_a], axis=1).astype(jnp.bfloat16)
    phase_b = (wave_step * lower_index)[None, :, None] * distance[:, None, :]
    table_b = jnp.concatenate([jnp.cos(phase_b), -jnp.sin(phase_b)], axis=1).astype(jnp.bfloat16)
    products = jnp.einsum('gan,gbn->gab', table_a.astype(jnp.float32), table_b.astype(jnp.float32))
    real_part = products[:, :BIN_HI, :BIN_LO] - products[:, BIN_HI:, BIN_LO:]
    imag_part = products[:, :BIN_HI, BIN_LO:] + products[:, BIN_HI:, :BIN_LO]
    return jnp.stack([real_part, imag_part]).reshape(2, antenna.shape[1], BINS)

def chirp_apply(spectrum, bin_rows, k_rows):
    offset_k = (k_rows - PULSES // 2).astype(jnp.float32)
    wave_bin = wave_start + wave_step * bin_rows.astype(jnp.float32)
    phase = jnp.pi * (offset_k * offset_k / PULSES)[None, :] * (wave_start / wave_bin)[:, None]
    cosine = jnp.cos(phase)
    sine_h = jnp.sin(phase)
    return jnp.stack([cosine * spectrum[0] - sine_h * spectrum[1], cosine * spectrum[1] + sine_h * spectrum[0]])

def reference(facet_positions, reflectivity, block_building, visible, platform):
    group_len = 8
    building_of = jnp.repeat(block_building, BLK)

    def one_group(group_index):
        first_pulse = group_index * group_len
        antenna = lax.dynamic_slice_in_dim(platform, first_pulse, group_len, 1)
        column = lax.dynamic_index_in_dim(visible, first_pulse // PBS, 1, keepdims=False)
        seen = jnp.take(column, building_of, axis=0).astype(jnp.float32)
        weights = reflectivity * seen[None, :]
        return echo_group(facet_positions, weights, antenna)
    groups = lax.map(one_group, jnp.arange(PULSES // group_len, dtype=jnp.int32))
    echo = groups.transpose(1, 3, 0, 2).reshape(2, BINS, PULSES)
    echo_b = echo.astype(jnp.bfloat16)
    k_rows = jnp.arange(PULSES, dtype=jnp.int32)
    angle_grid = 2.0 * math.pi / PULSES * (k_rows[:, None] * k_rows[None, :] % PULSES).astype(jnp.float32)
    scale_w = 1.0 / math.sqrt(PULSES)
    w_real = (jnp.cos(angle_grid) * scale_w).astype(jnp.bfloat16)
    w_imag = (-jnp.sin(angle_grid) * scale_w).astype(jnp.bfloat16)
    real_s = jnp.dot(echo_b[0], w_real.T, preferred_element_type=jnp.float32) - jnp.dot(echo_b[1], w_imag.T, preferred_element_type=jnp.float32)
    imag_s = jnp.dot(echo_b[0], w_imag.T, preferred_element_type=jnp.float32) + jnp.dot(echo_b[1], w_real.T, preferred_element_type=jnp.float32)
    spectrum = jnp.stack([real_s, imag_s])
    return chirp_apply(spectrum, jnp.arange(BINS, dtype=jnp.int32), k_rows)
```

```python
import functools
import math

import jax
import jax.numpy as jnp
import numpy as np
from jax import lax
from jax.experimental import pallas as pl
from jax.experimental.pallas import tpu as pltpu
from jax.sharding import PartitionSpec as P

BLK = 128
PBS = 32
BINS = 512
BIN_LO = 32
BIN_HI = 16
LANES = 128
ROWS = 32
STEP = 4
QUADS = 4


f32 = jnp.float32
bf16 = jnp.bfloat16

SIN_C = (4.442882878126042, -7.308239958462742, 3.606233657443361, -0.8453187380162854, 0.10822102663962477)
COS_C = (-1.4142135611352313, 6.978863916510845, -5.739875235214542, 1.8882041596407644, -0.33193097868538995, 0.03399741622323665)


def poly(coefs, w):
    acc = w * coefs[-1] + coefs[-2]
    for c in coefs[-3::-1]:
        acc = acc * w + c
    return acc


def cis_turns(v):
    w = v * v
    s = v * poly(SIN_C, w)
    c = poly(COS_C, w)
    return 1.0 - s * s, -(s * c)


def fold_matrix():
    out = np.zeros((2, 4, 32, 8, 2, 4, 32), np.float32)
    for tile in range(16):
        mp, cs, mi, sign = tile // 8, tile // 4 % 2, tile // 2 % 2, tile % 2
        for low in range(2):
            beta = 4 + 8 * (2 * mp + low) + (1, 3)[mi] * (1, -1)[sign]
            j = (beta - 1) // 2
            u = 2 * tile + low
            for al in range(4):
                if cs == 0:
                    for c in range(2):
                        out[c, al, u, :, c, al, 16 + j] = 1
                        out[c, al, u, :, c, al, 15 - j] = 1
                else:
                    out[1, al, u, :, 0, al, 16 + j] = 1
                    out[1, al, u, :, 0, al, 15 - j] = -1
                    out[0, al, u, :, 1, al, 16 + j] = -1
                    out[0, al, u, :, 1, al, 15 - j] = 1
    return out.reshape(2 * 4 * 32 * 8, 2 * 4 * 32)


def pack(low, high):
    return jnp.concatenate([low, high], axis=0).astype(bf16)


def block_tables(x, y, z, r0, r1, ax, ay, az):
    dx, dy, dz = x - ax, y - ay, z - az
    d2 = dx * dx + dy * dy + dz * dz
    t = d2 * lax.rsqrt(d2) * (1.0 / (16.0 * math.pi)) - 1.25
    w = t * t
    s = t * poly(SIN_C, w)
    c1 = s * poly(COS_C, w)
    s1 = 1.0 - s * s
    a2 = 4.0 * (c1 * c1) - 2.0
    c3, s3 = (a2 - 1.0) * c1, (a2 + 1.0) * s1
    c4, s4 = 0.5 * (a2 * a2) - 1.0, a2 * ((c1 + c1) * s1)
    a4 = c4 + c4
    a8, s8 = a4 * a4 - 2.0, a4 * s4
    c12, s12 = (a8 - 1.0) * c4, (a8 + 1.0) * s4
    c20, s20 = a8 * c12 - c4, a8 * s12 - s4
    c28, s28 = a8 * c20 - c12, a8 * s20 - s12
    a16, s16 = a8 * a8 - 2.0, a8 * s8
    a32, s32 = a16 * a16 - 2.0, a16 * s16
    a64, s64 = a32 * a32 - 2.0, a32 * s32
    a128, s128 = a64 * a64 - 2.0, a64 * s64
    a256, s256 = a128 * a128 - 2.0, a128 * s128
    c32 = 0.5 * a32
    c96, s96 = (a64 - 1.0) * c32, (a64 + 1.0) * s32
    c128, c16, c256 = 0.5 * a128, 0.5 * a16, 0.5 * a256
    c144, s144 = c128 * c16 - s128 * s16, s128 * c16 + c128 * s16
    c143, s143 = c144 * c1 + s144 * s1, s144 * c1 - c144 * s1
    q0r, q0i = r0 * c143 + r1 * s143, r1 * c143 - r0 * s143
    q1r, q1i = q0r * c256 + q0i * s256, q0i * c256 - q0r * s256
    q2r, q2i = a256 * q1r - q0r, a256 * q1i - q0i
    q3r, q3i = a256 * q2r - q1r, a256 * q2i - q1i
    a_tiles = []
    cm = [pack(c32, c32), pack(c96, c96)]
    sm = [pack(s32, s32), pack(s96, s96)]
    for qr, qi in ((pack(q0r, q1r), pack(q0i, q1i)), (pack(q2r, q3r), pack(q2i, q3i))):
        plus, minus = [], []
        for m in range(2):
            p1, p2, p3, p4 = qr * cm[m], qi * sm[m], qi * cm[m], qr * sm[m]
            plus.append((p1 + p2, p3 - p4))
            minus.append((p1 - p2, p3 + p4))
        for c in range(2):
            a_tiles += [minus[1][c], minus[0][c], plus[0][c], plus[1][c]]
    b_tiles = []
    cm = [pack(c1, c1), pack(c3, c3)]
    sm = [pack(s1, s1), pack(s3, s3)]
    for cl, sl in ((pack(c4, c12), pack(s4, s12)), (pack(c20, c28), pack(s20, s28))):
        cosines, sines = [], []
        for m in range(2):
            p1, p2, p3, p4 = cl * cm[m], sl * sm[m], sl * cm[m], cl * sm[m]
            cosines += [p1 - p2, p1 + p2]
            sines += [p3 + p4, p3 - p4]
        b_tiles += cosines + sines
    return jnp.concatenate(a_tiles, axis=0), jnp.concatenate(b_tiles, axis=0)


def echo_kernel(
    pieces, blocks, groups, buildings,
    words_ref, ant_ref, fac_ref, fold_hbm, out_ref,
    flags, flags_s, rows_s, counts_s, acc, products, fold, sem,
):
    fold_copy = pltpu.make_async_copy(fold_hbm, fold, sem.at[0])
    fold_copy.start()
    ids = fac_ref[pl.ds(ROWS - 2, pieces, stride=ROWS), :]
    marks = jnp.zeros(ids.shape, jnp.int32)
    for b in range(buildings):
        marks = jnp.where(ids == float(b), words_ref[b], marks)
    flags[...] = marks
    flag_copy = pltpu.make_async_copy(flags, flags_s, sem.at[1])
    flag_copy.start()
    flag_copy.wait()

    def list_piece(piece, counts):
        counts = list(counts)
        for j in range(blocks):
            word = flags_s[piece, j]
            for g in range(groups):
                rows_s[g, counts[g]] = piece * ROWS + j
                counts[g] = counts[g] + (lax.shift_right_logical(word, g) & 1)
        return tuple(counts)

    counts = lax.fori_loop(0, pieces, list_piece, (jnp.int32(0),) * groups)
    for g in range(groups):
        for extra in range(STEP - 1):
            rows_s[g, counts[g] + extra] = pieces * ROWS
        counts_s[g] = counts[g]
    rows8 = lax.broadcasted_iota(jnp.int32, (16, 256), 0) % 8
    same = rows8 == lax.broadcasted_iota(jnp.int32, (16, 256), 1) % 8

    def group(g, carry):
        base = pl.multiple_of(g * 8, 8)
        ax, ay, az = [
            jnp.broadcast_to(ant_ref[pl.ds(base, 8), i : i + 1], (8, LANES)) for i in range(3)
        ]
        acc[...] = jnp.zeros_like(acc)

        def step(i, carry):
            lefts, rights = [], []
            for j in range(STEP):
                row = rows_s[g, i * STEP + j]
                facet = [
                    fac_ref[pl.ds(row + blocks * c, 8, stride=0), :] for c in range(5)
                ]
                left, right = block_tables(*facet, ax, ay, az)
                lefts.append(left)
                rights.append(right)
            acc[...] += lax.dot_general(
                jnp.concatenate(lefts, axis=1), jnp.concatenate(rights, axis=1),
                (((1,), (1,)), ((), ())), preferred_element_type=f32,
            )
            return carry

        lax.fori_loop(0, lax.div(counts_s[g] + (STEP - 1), STEP), step, 0)
        for tile in range(16):
            hp, place = tile // 8, tile % 8
            kept = jnp.where(same, acc[tile * 16 : tile * 16 + 16, :], 0.0).astype(bf16)
            products[hp, g, :, place * 256 : place * 256 + 256] = kept
        return carry

    lax.fori_loop(0, groups, group, 0)
    fold_copy.wait()
    for hp in range(2):
        echo = jnp.dot(
            products[hp].reshape(groups * 16, 2048), fold[...], preferred_element_type=f32
        )
        for low in range(2):
            picked = [echo[g * 16 + low * 8 : g * 16 + low * 8 + 8] for g in range(groups)]
            out_ref[2 * hp + low] = jnp.concatenate(picked, axis=0).astype(bf16)


def echoes(facets, antenna, words, fold, pieces, blocks):
    groups = antenna.shape[0] // 8
    buildings = words.shape[0]
    most = pieces * blocks
    return pl.pallas_call(
        functools.partial(echo_kernel, pieces, blocks, groups, buildings),
        out_shape=jax.ShapeDtypeStruct((QUADS, groups * 8, 256), bf16),
        in_specs=[
            pl.BlockSpec(memory_space=pltpu.SMEM),
            pl.BlockSpec(memory_space=pltpu.VMEM),
            pl.BlockSpec(memory_space=pltpu.VMEM),
            pl.BlockSpec(memory_space=pl.ANY),
        ],
        out_specs=pl.BlockSpec(memory_space=pltpu.VMEM),
        scratch_shapes=[
            pltpu.VMEM((pieces, LANES), jnp.int32),
            pltpu.SMEM((pieces, LANES), jnp.int32),
            pltpu.SMEM((groups, most + STEP), jnp.int32),
            pltpu.SMEM((groups,), jnp.int32),
            pltpu.VMEM((256, 256), f32),
            pltpu.VMEM((2, groups, 16, 2048), bf16),
            pltpu.VMEM((2048, 256), bf16),
            pltpu.SemaphoreType.DMA((2,)),
        ],
        compiler_params=pltpu.CompilerParams(vmem_limit_bytes=16 << 20),
        name="echoes",
    )(words, antenna, facets, fold)


def transform_tables_kernel(
    facet_n, pulse_n, order, share, group_len, pulses, bins_dev, k_block,
    place_ref, w_ref, chirp_ref,
):
    mine_f, mine_z = place_ref[0], place_ref[1]
    k_ids = mine_f * k_block + lax.broadcasted_iota(jnp.int32, (k_block, LANES), 0)
    lane = lax.broadcasted_iota(jnp.int32, (k_block, LANES), 1)
    pulse_dev = pulses // pulse_n

    def rotation(index):
        back = (index + pulses // 2) % pulses - pulses // 2
        cosine, sine = cis_turns(back.astype(f32) * (1.0 / pulses))
        return cosine, -sine

    slot = lane // share
    within = lane % share
    here = (mine_z ^ (slot % pulse_n)) * pulse_dev + (
        within // group_len * facet_n + mine_f
    ) * group_len + within % group_len
    scale = 1.0 / math.sqrt(pulses)
    real, imag = rotation((k_ids * here) % pulses)
    wide = {0: (real * scale, imag * scale)}
    per_block = LANES // share
    turns = []
    bit = 1
    while bit < pulse_n:
        if bit >= per_block:
            sign = 1 - 2 * ((mine_z // bit) % 2)
            turns.append(sign * pulse_dev * bit)
        bit *= 2
    for bit in order:
        sign = 1 - 2 * ((mine_f // bit) % 2)
        turns.append(sign * group_len * bit)
    for level, turn in enumerate(turns):
        rr, ri = rotation((k_ids * turn) % pulses)
        for at in range(1 << level):
            real, imag = wide[at]
            wide[at + (1 << level)] = (real * rr - imag * ri, real * ri + imag * rr)
    for at, (real, imag) in wide.items():
        w_ref[:k_block, at * LANES : at * LANES + LANES] = real.astype(bf16)
        w_ref[k_block:, at * LANES : at * LANES + LANES] = imag.astype(bf16)
    offset = mine_f * k_block - pulses // 2 + lax.broadcasted_iota(jnp.int32, (k_block, bins_dev), 0)
    bins = mine_z * bins_dev + lax.broadcasted_iota(jnp.int32, (k_block, bins_dev), 1)
    phase = (offset * offset).astype(f32) * (8.0 / (2.0 * pulses)) / (8.0 + bins.astype(f32))
    cosine, sine = cis_turns(phase - jnp.round(phase))
    chirp_ref[0] = cosine
    chirp_ref[1] = sine


def transform_tables(place, facet_n, pulse_n, order, share, group_len, pulses, bins_dev, k_block):
    return pl.pallas_call(
        functools.partial(
            transform_tables_kernel, facet_n, pulse_n, order, share, group_len, pulses, bins_dev, k_block
        ),
        out_shape=(
            jax.ShapeDtypeStruct((2 * k_block, pulses), bf16),
            jax.ShapeDtypeStruct((2, k_block, bins_dev), f32),
        ),
        in_specs=[pl.BlockSpec(memory_space=pltpu.SMEM)],
        out_specs=(pl.BlockSpec(memory_space=pltpu.VMEM),) * 2,
        compiler_params=pltpu.CompilerParams(vmem_limit_bytes=16 << 20),
        name="transform_tables",
    )(place)


def transform_kernel(k_block, bins_dev, w_ref, chirp_ref, *refs):
    pieces, out_ref = refs[:-1], refs[-1]
    total = None
    at = 0
    for piece in pieces:
        rows = piece.shape[0]
        part = jnp.dot(w_ref[:, at : at + rows], piece[...], preferred_element_type=f32)
        total = part if total is None else total + part
        at += rows
    real = total[:k_block, :bins_dev] - total[k_block:, bins_dev:]
    imag = total[k_block:, :bins_dev] + total[:k_block, bins_dev:]
    cosine, sine = chirp_ref[0], chirp_ref[1]
    out_ref[0] = (cosine * real - sine * imag).T
    out_ref[1] = (cosine * imag + sine * real).T


def transform(w, chirp, pieces, k_block, bins_dev):
    return pl.pallas_call(
        functools.partial(transform_kernel, k_block, bins_dev),
        out_shape=jax.ShapeDtypeStruct((2, bins_dev, k_block), f32),
        in_specs=[pl.BlockSpec(memory_space=pltpu.VMEM)] * (2 + len(pieces)),
        out_specs=pl.BlockSpec(memory_space=pltpu.VMEM),
        compiler_params=pltpu.CompilerParams(vmem_limit_bytes=16 << 20),
        name="transform",
    )(w, chirp, *pieces)


def swap(x, axis, size, mask):
    return lax.ppermute(x, axis, [(i, i ^ mask) for i in range(size)])


def body(facet_positions, reflectivity, block_building, visible, platform):
    facet_n = lax.axis_size("facet")
    pulse_n = lax.axis_size("pulse")
    mine_f, mine_z = lax.axis_index("facet"), lax.axis_index("pulse")
    facets_here = facet_positions.shape[1]
    pulse_dev = platform.shape[1]
    pulses = pulse_dev * pulse_n
    blocks = facets_here // BLK
    share = pulse_dev // facet_n
    group_len = min(8, share)
    groups = share // group_len
    bins_dev = BINS // pulse_n
    k_block = pulses // facet_n
    buildings = visible.shape[0]

    ids = jnp.pad(block_building.astype(f32), (0, LANES - blocks), constant_values=-1.0)
    packed = jnp.concatenate([
        facet_positions.reshape(3 * blocks, BLK), reflectivity.reshape(2 * blocks, BLK),
        jnp.broadcast_to(ids, (ROWS - 5 * blocks, LANES)),
    ])
    away = [(i,) for i in range(1, facet_n)]
    facets = [packed]
    for mask in sorted(range(1, facet_n), key=lambda m: (-bin(m).count("1"), m)):
        facets.append(swap(packed, "facet", facet_n, mask))
    facets.append(jnp.zeros((ROWS, LANES), f32))
    facets = jnp.concatenate(facets)

    antenna = lax.dynamic_index_in_dim(
        platform.reshape(3, groups, facet_n, group_len), mine_f, 2, keepdims=False
    )
    antenna = jnp.pad(antenna, ((0, 0), (0, 0), (0, 8 - group_len)), mode="edge")
    antenna = antenna.reshape(3, groups * 8).T
    columns = (jnp.arange(groups) * facet_n + mine_f) * group_len
    column = (mine_z * pulse_dev + columns) // PBS
    if visible.shape[1] * PBS == pulse_dev:
        column = columns // PBS
    seen = jnp.take(visible, column, axis=1)
    words = jnp.sum(seen << jnp.arange(groups, dtype=jnp.int32)[None, :], axis=1)

    order = [1 << i for i in range(1, facet_n.bit_length() - 1)] + [1]
    place = jnp.stack([mine_f, mine_z]).astype(jnp.int32)
    w, chirp = transform_tables(
        place, facet_n, pulse_n, order, share, group_len, pulses, bins_dev, k_block
    )

    fold = jnp.asarray(fold_matrix(), bf16)
    echo = echoes(facets, antenna, words, fold, facet_n, blocks)

    echo = echo.reshape(QUADS, groups, 8, 2, LANES)[:, :, :group_len]
    if pulse_n > QUADS:
        echo = echo.reshape(QUADS, share, 2, pulse_n // QUADS, bins_dev).transpose(0, 3, 1, 2, 4)
    echo = echo.reshape(pulse_n, share, 2 * bins_dev)
    turned = [lax.dynamic_index_in_dim(echo, mine_z, 0, keepdims=False)]
    for mask in range(1, pulse_n):
        piece = lax.dynamic_index_in_dim(echo, mine_z ^ mask, 0, keepdims=False)
        turned.append(swap(piece, "pulse", pulse_n, mask))
    turned = jnp.concatenate(turned)

    near = [turned] + [swap(turned, "facet", facet_n, mask) for mask in range(2, facet_n, 2)]
    near = jnp.concatenate(near)
    far = swap(near, "facet", facet_n, 1)
    return transform(w, chirp, [near, far], k_block, bins_dev)


def solution(mesh):
    placed = (P(None, "facet"), P(None, "facet"), P("facet"), P(None, "pulse"), P(None, "pulse"))
    return jax.shard_map(
        body, mesh=mesh, in_specs=placed, out_specs=P(None, "pulse", "facet"), check_vma=False
    )
```

```python
import functools
import math

import jax
import jax.numpy as jnp
import numpy as np
from jax import lax
from jax.experimental import pallas as pl
from jax.experimental.pallas import tpu as pltpu
from jax.sharding import PartitionSpec as P

BLK = 128
PBS = 32
BINS = 512
BIN_LO = 32
BIN_HI = 16
LANES = 128
STEP = 4
ALL_VMEM = 67043328
QUADS = 4


f32 = jnp.float32
bf16 = jnp.bfloat16

SIN_C = (4.442882878126042, -7.308239958462742, 3.606233657443361, -0.8453187380162854, 0.10822102663962477)
COS_C = (-1.4142135611352313, 6.978863916510845, -5.739875235214542, 1.8882041596407644, -0.33193097868538995, 0.03399741622323665)


def poly(coefs, w):
    acc = w * coefs[-1] + coefs[-2]
    for c in coefs[-3::-1]:
        acc = acc * w + c
    return acc


def cis_turns(v):
    w = v * v
    s = v * poly(SIN_C, w)
    c = poly(COS_C, w)
    return 1.0 - s * s, -(s * c)


def fold_matrix():
    left = np.zeros((8, 2, 4))
    for m in range(2):
        plus, minus = (2 + m, 1 - m)
        for which, (c, sign) in enumerate(((0, 1), (0, 1), (1, 1), (1, -1))):
            left[m * 4 + which, c, plus] = sign
            left[m * 4 + which, c, minus] = (sign, -sign)[which % 2]
    right = np.zeros((16, 2, 2, 16))
    for mp in range(2):
        for m in range(2):
            for low in range(2):
                middle, off = 4 + 8 * (2 * mp + low), (1, 3)[m]
                for which, (cs, plus, minus) in enumerate(((0, 1, 1), (0, -1, 1), (1, 1, 1), (1, 1, -1))):
                    right[mp * 8 + m * 4 + which, low, cs, (middle + off - 1) // 2] = plus
                    right[mp * 8 + m * 4 + which, low, cs, (middle - off - 1) // 2] = minus
    both = np.einsum("tca,ulsj->tulcsaj", left, right)
    out = np.zeros((8, 16, 2, 2, 4, 32))
    up, down = slice(16, 32), slice(15, None, -1)
    out[:, :, :, 0, :, up] = both[:, :, :, 0, 0] + both[:, :, :, 1, 1]
    out[:, :, :, 0, :, down] = both[:, :, :, 0, 0] - both[:, :, :, 1, 1]
    out[:, :, :, 1, :, up] = both[:, :, :, 1, 0] - both[:, :, :, 0, 1]
    out[:, :, :, 1, :, down] = both[:, :, :, 1, 0] + both[:, :, :, 0, 1]
    return out.reshape(8 * 32, 2 * 4 * 32)


def pack(low, high):
    return jnp.concatenate([low, high], axis=0).astype(bf16)


def block_factors(x, y, z, r0, r1, ax, ay, az):
    dx, dy, dz = x - ax, y - ay, z - az
    d2 = dx * dx + dy * dy + dz * dz
    t = d2 * lax.rsqrt(d2) - 1.25
    w = t * t
    s = t * poly(SIN_C, w)
    c1 = s * poly(COS_C, w)
    s1 = 1.0 - s * s
    a2 = 4.0 * (c1 * c1) - 2.0
    c3, s3 = (a2 - 1.0) * c1, (a2 + 1.0) * s1
    a4, s4 = a2 * a2 - 2.0, a2 * ((c1 + c1) * s1)
    c4 = 0.5 * a4
    a8, s8 = a4 * a4 - 2.0, a4 * s4
    c12, s12 = (a8 - 1.0) * c4, (a8 + 1.0) * s4
    c20, s20 = a8 * c12 - c4, a8 * s12 - s4
    c28, s28 = a8 * c20 - c12, a8 * s20 - s12
    a16, s16 = a8 * a8 - 2.0, a8 * s8
    a32, s32 = a16 * a16 - 2.0, a16 * s16
    a64, s64 = a32 * a32 - 2.0, a32 * s32
    a128, s128 = a64 * a64 - 2.0, a64 * s64
    a256, s256 = a128 * a128 - 2.0, a128 * s128
    c32 = 0.5 * a32
    c96, s96 = (a64 - 1.0) * c32, (a64 + 1.0) * s32
    c128, c16, c256 = 0.5 * a128, 0.5 * a16, 0.5 * a256
    c144, s144 = c128 * c16 - s128 * s16, s128 * c16 + c128 * s16
    c143, s143 = c144 * c1 + s144 * s1, s144 * c1 - c144 * s1
    q0r, q0i = r0 * c143 + r1 * s143, r1 * c143 - r0 * s143
    q1r, q1i = q0r * c256 + q0i * s256, q0i * c256 - q0r * s256
    q2r, q2i = a256 * q1r - q0r, a256 * q1i - q0i
    q3r, q3i = a256 * q2r - q1r, a256 * q2i - q1i
    return (
        c32, s32, c96, s96, q0r, q0i, q1r, q1i, q2r, q2i, q3r, q3i,
        c1, s1, c3, s3, c4, s4, c12, s12, c20, s20, c28, s28,
    )


def table_of(factors):
    near, far = factors[:4], factors[4:]
    near = [pack(value, value) for value in near]
    tiles = []
    for low in (0, 4):
        real, imag = pack(far[low], far[low + 2]), pack(far[low + 1], far[low + 3])
        for cosine, sine in (near[0:2], near[2:4]):
            tiles += [real * cosine, imag * sine, imag * cosine, real * sine]
    return jnp.concatenate(tiles, axis=0)


def echo_kernel(
    pieces, blocks, groups, group_len, buildings,
    words_ref, platform_ref, fold, *refs,
):
    piece_refs = refs[:pieces]
    out_ref, fac_ref, marks_v, marks_s, rows_s, antenna, factors, products, sem = refs[pieces:]
    mine = lax.axis_index("facet")
    in_turns = 1.0 / (16.0 * math.pi)
    scale = jnp.where(lax.broadcasted_iota(jnp.int32, (8, LANES), 0) < 3, in_turns, 1.0)
    for piece, ref in enumerate(piece_refs):
        for j in range(blocks):
            at = (piece * blocks + j) * 8
            fac_ref[at : at + 8, :] = ref[:, j * LANES : j * LANES + LANES] * scale
    fac_ref[pieces * blocks * 8 :, :] = jnp.zeros((8, LANES), f32)
    ids = jnp.concatenate([ref[5:6, :LANES] for ref in piece_refs], axis=0)
    marks = jnp.zeros(ids.shape, jnp.int32)
    for b in range(buildings):
        marks = jnp.where(ids == float(b), words_ref[b], marks)
    marks_v[:pieces, :] = marks
    marks_v[pieces:, :] = jnp.zeros((8, LANES), jnp.int32)
    marks_copy = pltpu.make_async_copy(marks_v, marks_s, sem)
    marks_copy.start()
    pulse_dev = platform_ref.shape[1]
    flat = platform_ref[...]
    flat = jnp.concatenate([flat, jnp.zeros((8 - flat.shape[0], pulse_dev), f32)], axis=0)
    antenna[:pulse_dev, :8] = flat.T
    antenna[pulse_dev:, :] = jnp.zeros((8, LANES), f32)
    marks_copy.wait()
    most = pieces * blocks + 2 * STEP

    def scan(piece, g, at):
        for j in range(blocks):
            rows_s[at] = (piece * blocks + j) * 8
            at = at + (lax.shift_right_logical(marks_s[piece, j], g) & 1)
        return at

    def close(at):
        for extra in range(2 * STEP):
            rows_s[at + extra] = pieces * blocks * 8

    def station(g):
        g = jnp.minimum(g, groups - 1)
        ant = antenna[pl.ds((g * pieces + mine) * group_len, 8), :]
        return [jnp.broadcast_to(ant[:, i : i + 1], (8, LANES)) for i in range(3)]

    def prepare(at, place):
        for j in range(STEP):
            row = rows_s[at + j]
            facet = [fac_ref[pl.ds(row + c, 8, stride=0), :] for c in range(5)]
            for k, tile in enumerate(block_factors(*facet, *place)):
                factors[j, k] = tile

    same = (
        lax.broadcasted_iota(jnp.int32, (16, 256), 0) % 8
        == lax.broadcasted_iota(jnp.int32, (16, 256), 1) % 8
    )

    def group(acc0, acc1, g, count):
        place = station(g)
        here, there = (g % 2) * most, ((g + 1) % 2) * most
        steps = jnp.maximum(lax.div(count + (STEP - 1), STEP), 1)

        def step(i, at):
            for half, acc in ((0, acc0), (1, acc1)):
                pair = [[factors[2 * half + j, k] for k in range(24)] for j in range(2)]
                left = jnp.concatenate([table_of(p[:12]) for p in pair], axis=1)
                right = jnp.concatenate([table_of(p[12:]) for p in pair], axis=1)
                pltpu.matmul_push_rhs(right, staging_register=0, mxu_index=half, transpose=True)
                pltpu.matmul_acc_lhs(acc, left, load_staged_rhs=0)
            prepare(here + (i + 1) * STEP, place)
            return scan(jnp.minimum(i, pieces), g + 1, at)

        at = lax.fori_loop(0, steps, step, there)
        at = lax.fori_loop(
            jnp.minimum(steps, pieces), pieces, lambda piece, n: scan(piece, g + 1, n), at
        )
        close(at)
        prepare(there, station(g + 1))
        total = pltpu.matmul_pop(acc0) + pltpu.matmul_pop(acc1)
        for tile in range(16):
            hp, spot = tile // 8, tile % 8
            kept = jnp.where(same, total[tile * 16 : tile * 16 + 16, :], 0.0).astype(bf16)
            products[hp, pl.ds(pl.multiple_of(g * 16, 16), 16), spot * 256 : spot * 256 + 256] = kept
        return at - there

    first = lax.fori_loop(0, pieces, lambda piece, n: scan(piece, 0, n), jnp.int32(0))
    close(first)
    prepare(0, station(0))
    pl.run_scoped(
        lambda acc0, acc1: lax.fori_loop(0, groups, functools.partial(group, acc0, acc1), first),
        pltpu.ACC(0)((256, 256), f32), pltpu.ACC(1)((256, 256), f32),
    )
    pl.run_scoped(
        functools.partial(fold_products, groups, products, fold, out_ref),
        pltpu.ACC(0)((groups * 16, 256), f32), pltpu.ACC(1)((groups * 16, 256), f32),
    )


def fold_products(groups, products, fold, out_ref, *accs):
    for k in range(8):
        lanes = slice(k * 256, k * 256 + 256)
        for hp, acc in enumerate(accs):
            pltpu.matmul_push_rhs(fold[lanes, :], staging_register=k % 2, mxu_index=hp)
            pltpu.matmul_acc_lhs(acc, products[hp, :, lanes], load_staged_rhs=k % 2)
    for hp, acc in enumerate(accs):
        echo = pltpu.matmul_pop(acc)
        for low in range(2):
            picked = [echo[g * 16 + low * 8 : g * 16 + low * 8 + 8] for g in range(groups)]
            out_ref[2 * hp + low] = jnp.concatenate(picked, axis=0).astype(bf16)


def echoes(words, platform, fold, facets, blocks, groups, group_len):
    pieces = len(facets)
    most = pieces * blocks + 2 * STEP
    pulse_dev = platform.shape[1]
    vmem = pl.BlockSpec(memory_space=pltpu.VMEM)
    return pl.pallas_call(
        functools.partial(echo_kernel, pieces, blocks, groups, group_len, words.shape[0]),
        out_shape=jax.ShapeDtypeStruct((QUADS, groups * 8, 256), bf16),
        in_specs=[pl.BlockSpec(memory_space=pltpu.SMEM), vmem, vmem] + [vmem] * pieces,
        out_specs=vmem,
        scratch_shapes=[
            pltpu.VMEM(((pieces * blocks + 1) * 8, LANES), f32),
            pltpu.VMEM((pieces + 8, LANES), jnp.int32),
            pltpu.SMEM((pieces + 8, LANES), jnp.int32),
            pltpu.SMEM((2 * most + 2 * STEP,), jnp.int32),
            pltpu.VMEM((pulse_dev + 8, LANES), f32),
            pltpu.VMEM((STEP, 24, 8, LANES), f32),
            pltpu.VMEM((2, groups * 16, 2048), bf16),
            pltpu.SemaphoreType.DMA,
        ],
        compiler_params=pltpu.CompilerParams(vmem_limit_bytes=16 << 20),
        name="echoes",
    )(words, platform, fold, *facets)


def pack_kernel(ids_hbm, positions_hbm, reflectivity_hbm, out_ref, ids, positions, reflectivity, sems):
    copies = [
        pltpu.make_async_copy(source, target, sems.at[i])
        for i, (source, target) in enumerate((
            (positions_hbm, positions), (reflectivity_hbm, reflectivity), (ids_hbm, ids)
        ))
    ]
    for copy in copies:
        copy.start()
    for copy in copies:
        copy.wait()
    lane = lax.broadcasted_iota(jnp.int32, (3, LANES), 1)
    row = jnp.zeros(lane.shape, f32)
    for j in range(ids.shape[0]):
        row = jnp.where(lane == j, ids[j].astype(f32), row)
    out_ref[0:3, :] = positions[...]
    out_ref[3:5, :] = reflectivity[...]
    out_ref[5:8, :LANES] = row
    out_ref[5:8, LANES:] = jnp.zeros((3, out_ref.shape[1] - LANES), f32)


def pack_facets(ids, positions, reflectivity):
    return pl.pallas_call(
        pack_kernel,
        out_shape=jax.ShapeDtypeStruct((8, positions.shape[1]), f32),
        in_specs=[pl.BlockSpec(memory_space=pl.ANY)] * 3,
        out_specs=pl.BlockSpec(memory_space=pltpu.VMEM),
        scratch_shapes=[
            pltpu.SMEM(ids.shape, jnp.int32),
            pltpu.VMEM(positions.shape, f32),
            pltpu.VMEM(reflectivity.shape, f32),
            pltpu.SemaphoreType.DMA((3,)),
        ],
        compiler_params=pltpu.CompilerParams(vmem_limit_bytes=ALL_VMEM),
        name="pack_facets",
    )(ids, positions, reflectivity)


def transform_tables_kernel(
    facet_n, pulse_n, order, share, group_len, pulses, bins_dev, k_block,
    after_ref, w_ref, chirp_ref,
):
    mine_f, mine_z = lax.axis_index("facet"), lax.axis_index("pulse")
    k_ids = mine_f * k_block + lax.broadcasted_iota(jnp.int32, (k_block, LANES), 0)
    lane = lax.broadcasted_iota(jnp.int32, (k_block, LANES), 1)
    pulse_dev = pulses // pulse_n

    def rotation(index):
        back = (index + pulses // 2) % pulses - pulses // 2
        cosine, sine = cis_turns(back.astype(f32) * (1.0 / pulses))
        return cosine, -sine

    slot = lane // share
    within = lane % share
    here = (mine_z ^ (slot % pulse_n)) * pulse_dev + (
        within // group_len * facet_n + mine_f
    ) * group_len + within % group_len
    scale = 1.0 / math.sqrt(pulses)
    real, imag = rotation((k_ids * here) % pulses)
    wide = {0: (real * scale, imag * scale)}
    per_block = LANES // share
    turns = []
    bit = 1
    while bit < pulse_n:
        if bit >= per_block:
            sign = 1 - 2 * ((mine_z // bit) % 2)
            turns.append(sign * pulse_dev * bit)
        bit *= 2
    for bit in order:
        sign = 1 - 2 * ((mine_f // bit) % 2)
        turns.append(sign * group_len * bit)
    for level, turn in enumerate(turns):
        rr, ri = rotation((k_ids * turn) % pulses)
        for at in range(1 << level):
            real, imag = wide[at]
            wide[at + (1 << level)] = (real * rr - imag * ri, real * ri + imag * rr)
    for at, (real, imag) in wide.items():
        w_ref[:k_block, at * LANES : at * LANES + LANES] = real.astype(bf16)
        w_ref[k_block:, at * LANES : at * LANES + LANES] = imag.astype(bf16)
    offset = mine_f * k_block - pulses // 2 + lax.broadcasted_iota(jnp.int32, (k_block, bins_dev), 0)
    bins = mine_z * bins_dev + lax.broadcasted_iota(jnp.int32, (k_block, bins_dev), 1)
    phase = (offset * offset).astype(f32) * (8.0 / (2.0 * pulses)) / (8.0 + bins.astype(f32))
    cosine, sine = cis_turns(phase - jnp.round(phase))
    chirp_ref[0] = cosine
    chirp_ref[1] = sine


def transform_tables(after, facet_n, pulse_n, order, share, group_len, pulses, bins_dev, k_block):
    return pl.pallas_call(
        functools.partial(
            transform_tables_kernel, facet_n, pulse_n, order, share, group_len, pulses, bins_dev, k_block
        ),
        out_shape=(
            jax.ShapeDtypeStruct((2 * k_block, pulses), bf16),
            jax.ShapeDtypeStruct((2, k_block, bins_dev), f32),
        ),
        in_specs=[pl.BlockSpec(memory_space=pl.ANY)],
        out_specs=(pl.BlockSpec(memory_space=pltpu.VMEM),) * 2,
        compiler_params=pltpu.CompilerParams(vmem_limit_bytes=16 << 20),
        name="transform_tables",
    )(after)


def transform_kernel(k_block, bins_dev, w_ref, chirp_ref, *refs):
    pieces, out_ref = refs[:-1], refs[-1]
    total = None
    at = 0
    for piece in pieces:
        rows = piece.shape[0]
        part = jnp.dot(w_ref[:, at : at + rows], piece[...], preferred_element_type=f32)
        total = part if total is None else total + part
        at += rows
    real = total[:k_block, :bins_dev] - total[k_block:, bins_dev:]
    imag = total[k_block:, :bins_dev] + total[:k_block, bins_dev:]
    cosine, sine = chirp_ref[0], chirp_ref[1]
    out_ref[0] = (cosine * real - sine * imag).T
    out_ref[1] = (cosine * imag + sine * real).T


def transform(w, chirp, pieces, k_block, bins_dev):
    return pl.pallas_call(
        functools.partial(transform_kernel, k_block, bins_dev),
        out_shape=jax.ShapeDtypeStruct((2, bins_dev, k_block), f32),
        in_specs=[pl.BlockSpec(memory_space=pltpu.VMEM)] * (2 + len(pieces)),
        out_specs=pl.BlockSpec(memory_space=pltpu.VMEM),
        compiler_params=pltpu.CompilerParams(vmem_limit_bytes=16 << 20),
        name="transform",
    )(w, chirp, *pieces)


def swap(x, axis, size, mask):
    return lax.ppermute(x, axis, [(i, i ^ mask) for i in range(size)])


def gather_facet(x, size):
    near = [x] + [swap(x, "facet", size, mask) for mask in range(size - 2, 0, -2)]
    near = [near[0]] + near[:0:-1]
    out = []
    for piece in near:
        out += [piece, swap(piece, "facet", size, 1)]
    return out


def body(facet_positions, reflectivity, block_building, visible, platform):
    facet_n = lax.axis_size("facet")
    pulse_n = lax.axis_size("pulse")
    mine_z = lax.axis_index("pulse")
    pulse_dev = platform.shape[1]
    pulses = pulse_dev * pulse_n
    blocks = facet_positions.shape[1] // BLK
    share = pulse_dev // facet_n
    group_len = min(8, share)
    groups = share // group_len
    bins_dev = BINS // pulse_n
    k_block = pulses // facet_n

    packed = pack_facets(block_building, facet_positions, reflectivity)
    facets = gather_facet(packed, facet_n)

    mine_f = lax.axis_index("facet")
    columns = (jnp.arange(groups, dtype=jnp.int32) * facet_n + mine_f) * group_len // PBS
    bits = jnp.left_shift(jnp.int32(1), jnp.arange(groups, dtype=jnp.int32))
    there = jnp.arange(visible.shape[1], dtype=jnp.int32)[:, None] == columns[None, :]
    weights = jnp.sum(jnp.where(there, bits[None, :], 0), axis=1)
    words = jnp.sum(visible * weights[None, :], axis=1)
    stations = platform * (1.0 / (16.0 * math.pi))
    one = (mine_f >= 0).astype(bf16)
    fold = jnp.broadcast_to(jnp.asarray(fold_matrix(), bf16)[:, None, :], (256, 8, 256)) * one
    fold = fold.reshape(2048, 256)

    echo = echoes(words, stations, fold, facets, blocks, groups, group_len)
    order = [1 << i for i in range(facet_n.bit_length() - 1)]
    w, chirp = transform_tables(
        echo, facet_n, pulse_n, order, share, group_len, pulses, bins_dev, k_block
    )

    echo = echo.reshape(QUADS, groups, 8, 2, LANES)[:, :, :group_len]
    if pulse_n > QUADS:
        echo = echo.reshape(QUADS, share, 2, pulse_n // QUADS, bins_dev).transpose(0, 3, 1, 2, 4)
    echo = echo.reshape(pulse_n, share, 2 * bins_dev)
    turned = [lax.dynamic_index_in_dim(echo, mine_z, 0, keepdims=False)]
    for mask in range(1, pulse_n):
        piece = lax.dynamic_index_in_dim(echo, mine_z ^ mask, 0, keepdims=False)
        turned.append(swap(piece, "pulse", pulse_n, mask))
    turned, w, chirp = lax.optimization_barrier((jnp.concatenate(turned), w, chirp))

    pieces = gather_facet(turned, facet_n)
    return transform(w, chirp, pieces, k_block, bins_dev)


def solution(mesh):
    placed = (P(None, "facet"), P(None, "facet"), P("facet"), P(None, "pulse"), P(None, "pulse"))
    return jax.shard_map(
        body, mesh=mesh, in_specs=placed, out_specs=P(None, "pulse", "facet"), check_vma=False
    )
```

```python
import functools
import math

import jax
import jax.numpy as jnp
import numpy as np
from jax import lax
from jax.experimental import pallas as pl
from jax.experimental.pallas import tpu as pltpu
from jax.sharding import PartitionSpec as P

BLK = 128
PBS = 32
BINS = 512
BIN_LO = 32
BIN_HI = 16
LANES = 128
STEP = 4
ALL_VMEM = 67043328
QUADS = 4


f32 = jnp.float32
bf16 = jnp.bfloat16

SIN_C = (4.442882878126042, -7.308239958462742, 3.606233657443361, -0.8453187380162854, 0.10822102663962477)
COS_C = (-1.4142135611352313, 6.978863916510845, -5.739875235214542, 1.8882041596407644, -0.33193097868538995, 0.03399741622323665)


def poly(coefs, w):
    acc = w * coefs[-1] + coefs[-2]
    for c in coefs[-3::-1]:
        acc = acc * w + c
    return acc


def cis_turns(v):
    w = v * v
    s = v * poly(SIN_C, w)
    c = poly(COS_C, w)
    return 1.0 - s * s, -(s * c)


def fold_matrix():
    left = np.zeros((8, 2, 4))
    for m in range(2):
        plus, minus = (2 + m, 1 - m)
        for which, (c, sign) in enumerate(((0, 1), (0, 1), (1, 1), (1, -1))):
            left[m * 4 + which, c, plus] = sign
            left[m * 4 + which, c, minus] = (sign, -sign)[which % 2]
    right = np.zeros((16, 2, 2, 16))
    for mp in range(2):
        for m in range(2):
            for low in range(2):
                middle, off = 4 + 8 * (2 * mp + low), (1, 3)[m]
                for which, (cs, plus, minus) in enumerate(((0, 1, 1), (0, -1, 1), (1, 1, 1), (1, 1, -1))):
                    right[mp * 8 + m * 4 + which, low, cs, (middle + off - 1) // 2] = plus
                    right[mp * 8 + m * 4 + which, low, cs, (middle - off - 1) // 2] = minus
    both = np.einsum("tca,ulsj->tulcsaj", left, right)
    out = np.zeros((8, 16, 2, 2, 4, 32))
    up, down = slice(16, 32), slice(15, None, -1)
    out[:, :, :, 0, :, up] = both[:, :, :, 0, 0] + both[:, :, :, 1, 1]
    out[:, :, :, 0, :, down] = both[:, :, :, 0, 0] - both[:, :, :, 1, 1]
    out[:, :, :, 1, :, up] = both[:, :, :, 1, 0] - both[:, :, :, 0, 1]
    out[:, :, :, 1, :, down] = both[:, :, :, 1, 0] + both[:, :, :, 0, 1]
    return out.reshape(8 * 32, 2 * 4 * 32) / 16.0


def pack(low, high):
    return jnp.concatenate([low, high], axis=0).astype(bf16)


def block_angles(x, y, z, ax, ay, az):
    dx, dy, dz = x - ax, y - ay, z - az
    d2 = dx * dx + dy * dy + dz * dz
    t = d2 * lax.rsqrt(d2) - 1.25
    w = t * t
    s = t * poly(SIN_C, w)
    return s * poly(COS_C, w), 1.0 - s * s


def block_factors(c1, s1, r0, r1):
    square = c1 * c1
    a2, b2 = 4.0 * square - 2.0, 4.0 * (c1 * s1)
    c3, s3 = (a2 - 1.0) * c1, (a2 + 1.0) * s1
    a4, b4 = a2 * a2 - 2.0, a2 * b2
    a8, b8 = a4 * a4 - 2.0, a4 * b4
    a12, b12 = (a8 - 1.0) * a4, (a8 + 1.0) * b4
    a20, b20 = a8 * a12 - a4, a8 * b12 - b4
    a28, b28 = a8 * a20 - a12, a8 * b20 - b12
    a16, b16 = a8 * a8 - 2.0, a8 * b8
    a32, b32 = a16 * a16 - 2.0, a16 * b16
    a64, b64 = a32 * a32 - 2.0, a32 * b32
    a128, b128 = a64 * a64 - 2.0, a64 * b64
    a256, b256 = a128 * a128 - 2.0, a128 * b128
    a96, b96 = (a64 - 1.0) * a32, (a64 + 1.0) * b32
    c256, s256 = 0.5 * a256, 0.5 * b256
    c144, s144 = a128 * a16 - b128 * b16, b128 * a16 + a128 * b16
    c143, s143 = c144 * c1 + s144 * s1, s144 * c1 - c144 * s1
    q0r, q0i = r0 * c143 + r1 * s143, r1 * c143 - r0 * s143
    q1r, q1i = q0r * c256 + q0i * s256, q0i * c256 - q0r * s256
    q2r, q2i = a256 * q1r - q0r, a256 * q1i - q0i
    q3r, q3i = a256 * q2r - q1r, a256 * q2i - q1i
    return (
        a32, b32, a96, b96, q0r, q0i, q1r, q1i, q2r, q2i, q3r, q3i,
        c1, s1, c3, s3, a4, b4, a12, b12, a20, b20, a28, b28,
    )


def table_of(factors):
    near, far = factors[:4], factors[4:]
    near = [pack(value, value) for value in near]
    tiles = []
    for low in (0, 4):
        real, imag = pack(far[low], far[low + 2]), pack(far[low + 1], far[low + 3])
        for cosine, sine in (near[0:2], near[2:4]):
            tiles += [real * cosine, imag * sine, imag * cosine, real * sine]
    return jnp.concatenate(tiles, axis=0)


def echo_kernel(
    pieces, blocks, groups, group_len, buildings,
    platform_ref, fold, *refs,
):
    piece_refs = refs[:pieces]
    out_ref, fac_ref, marks_v, marks_s, rows_s, antenna, angles, products, sem = refs[pieces:]
    mine = lax.axis_index("facet")
    in_turns = 1.0 / (16.0 * math.pi)
    scale = jnp.where(lax.broadcasted_iota(jnp.int32, (8, LANES), 0) < 3, in_turns, 1.0)
    for piece, ref in enumerate(piece_refs):
        for j in range(blocks):
            at = (piece * blocks + j) * 8
            fac_ref[at : at + 8, :] = ref[:, j * LANES : j * LANES + LANES] * scale
    fac_ref[pieces * blocks * 8 :, :] = jnp.zeros((8, LANES), f32)
    ids = jnp.concatenate([ref[5:6, :LANES] for ref in piece_refs], axis=0)
    marks = jnp.zeros(ids.shape, jnp.int32)
    for b in range(buildings):
        marks = jnp.where(ids == float(b), piece_refs[0][6:7, b : b + 1].astype(jnp.int32), marks)
    marks_v[:pieces, :] = marks
    marks_v[pieces:, :] = jnp.zeros((8, LANES), jnp.int32)
    marks_copy = pltpu.make_async_copy(marks_v, marks_s, sem)
    marks_copy.start()
    pulse_dev = platform_ref.shape[1]
    flat = platform_ref[...]
    flat = jnp.concatenate([flat, jnp.zeros((8 - flat.shape[0], pulse_dev), f32)], axis=0)
    antenna[:pulse_dev, :8] = flat.T
    antenna[pulse_dev:, :] = jnp.zeros((8, LANES), f32)
    marks_copy.wait()
    most = pieces * blocks + 3 * STEP

    def scan(piece, g, at):
        for j in range(blocks):
            rows_s[at] = (piece * blocks + j) * 8
            at = at + (lax.shift_right_logical(marks_s[piece, j], g) & 1)
        return at

    def close(at):
        for extra in range(3 * STEP):
            rows_s[at + extra] = pieces * blocks * 8

    def station(g):
        g = jnp.minimum(g, groups - 1)
        ant = antenna[pl.ds((g * pieces + mine) * group_len, 8), :]
        return [jnp.broadcast_to(ant[:, i : i + 1], (8, LANES)) for i in range(3)]

    def turn(at, place):
        for j in range(STEP):
            row = rows_s[at + j]
            facet = [fac_ref[pl.ds(row + c, 8, stride=0), :] for c in range(3)]
            angles[j, 0], angles[j, 1] = block_angles(*facet, *place)

    def read(at, j):
        row = rows_s[at + j]
        weights = [fac_ref[pl.ds(row + c, 8, stride=0), :] for c in (3, 4)]
        return angles[j, 0], angles[j, 1], *weights

    same = (
        lax.broadcasted_iota(jnp.int32, (16, 256), 0) % 8
        == lax.broadcasted_iota(jnp.int32, (16, 256), 1) % 8
    )

    def group(acc0, acc1, g, count):
        place = station(g)
        here, there = (g % 2) * most, ((g + 1) % 2) * most
        steps = jnp.maximum(lax.div(count + (STEP - 1), STEP), 1)

        def step(i, at):
            for half, acc in ((0, acc0), (1, acc1)):
                pair = [block_factors(*read(here + i * STEP, 2 * half + j)) for j in range(2)]
                right = jnp.concatenate([table_of(p[12:]) for p in pair], axis=1)
                left = jnp.concatenate([table_of(p[:12]) for p in pair], axis=1)
                pltpu.matmul_push_rhs(right, staging_register=0, mxu_index=half, transpose=True)
                pltpu.matmul_acc_lhs(acc, left, load_staged_rhs=0)
            turn(here + (i + 1) * STEP, place)
            return scan(jnp.minimum(i, pieces), g + 1, at)

        at = lax.fori_loop(0, steps, step, there)
        at = lax.fori_loop(
            jnp.minimum(steps, pieces), pieces, lambda piece, n: scan(piece, g + 1, n), at
        )
        close(at)
        turn(there, station(g + 1))
        total = pltpu.matmul_pop(acc0) + pltpu.matmul_pop(acc1)
        for tile in range(16):
            hp, spot = tile // 8, tile % 8
            kept = jnp.where(same, total[tile * 16 : tile * 16 + 16, :], 0.0).astype(bf16)
            products[hp, pl.ds(pl.multiple_of(g * 16, 16), 16), spot * 256 : spot * 256 + 256] = kept
        return at - there

    first = lax.fori_loop(0, pieces, lambda piece, n: scan(piece, 0, n), jnp.int32(0))
    close(first)
    turn(0, station(0))
    pl.run_scoped(
        lambda acc0, acc1: lax.fori_loop(0, groups, functools.partial(group, acc0, acc1), first),
        pltpu.ACC(0)((256, 256), f32), pltpu.ACC(1)((256, 256), f32),
    )
    pl.run_scoped(
        functools.partial(fold_products, groups, products, fold, out_ref),
        pltpu.ACC(0)((groups * 16, 256), f32), pltpu.ACC(1)((groups * 16, 256), f32),
    )


def fold_products(groups, products, fold, out_ref, *accs):
    for k in range(8):
        lanes = slice(k * 256, k * 256 + 256)
        for hp, acc in enumerate(accs):
            pltpu.matmul_push_rhs(fold[lanes, :], staging_register=k % 2, mxu_index=hp)
            pltpu.matmul_acc_lhs(acc, products[hp, :, lanes], load_staged_rhs=k % 2)
    for hp, acc in enumerate(accs):
        echo = pltpu.matmul_pop(acc)
        for low in range(2):
            picked = [echo[g * 16 + low * 8 : g * 16 + low * 8 + 8] for g in range(groups)]
            out_ref[2 * hp + low] = jnp.concatenate(picked, axis=0).astype(bf16)


def echoes(buildings, platform, fold, facets, blocks, groups, group_len):
    pieces = len(facets)
    most = pieces * blocks + 3 * STEP
    pulse_dev = platform.shape[1]
    vmem = pl.BlockSpec(memory_space=pltpu.VMEM)
    return pl.pallas_call(
        functools.partial(echo_kernel, pieces, blocks, groups, group_len, buildings),
        out_shape=jax.ShapeDtypeStruct((QUADS, groups * 8, 256), bf16),
        in_specs=[vmem] * (2 + pieces),
        out_specs=vmem,
        scratch_shapes=[
            pltpu.VMEM(((pieces * blocks + 1) * 8, LANES), f32),
            pltpu.VMEM((pieces + 8, LANES), jnp.int32),
            pltpu.SMEM((pieces + 8, LANES), jnp.int32),
            pltpu.SMEM((2 * most + 3 * STEP,), jnp.int32),
            pltpu.VMEM((pulse_dev + 8, LANES), f32),
            pltpu.VMEM((STEP, 2, 8, LANES), f32),
            pltpu.VMEM((2, groups * 16, 2048), bf16),
            pltpu.SemaphoreType.DMA,
        ],
        compiler_params=pltpu.CompilerParams(vmem_limit_bytes=16 << 20),
        name="echoes",
    )(platform, fold, *facets)


def pack_kernel(
    groups, group_len, ids_hbm, positions_hbm, reflectivity_hbm, visible_hbm, out_ref,
    ids, positions, reflectivity, visible, sems,
):
    mine, count = lax.axis_index("facet"), lax.axis_size("facet")
    copies = [
        pltpu.make_async_copy(source, target, sems.at[i])
        for i, (source, target) in enumerate((
            (visible_hbm, visible), (ids_hbm, ids),
            (positions_hbm, positions), (reflectivity_hbm, reflectivity),
        ))
    ]
    for copy in copies:
        copy.start()
    for copy in copies:
        copy.wait()
    lane = lax.broadcasted_iota(jnp.int32, (1, LANES), 1)
    row = jnp.zeros(lane.shape, f32)
    for j in range(ids.shape[0]):
        row = jnp.where(lane == j, ids[j].astype(f32), row)
    words = jnp.zeros(lane.shape, jnp.int32)
    columns = [lax.div((g * count + mine) * group_len, PBS) for g in range(groups)]
    for b in range(visible.shape[0]):
        word = jnp.int32(0)
        for g, column in enumerate(columns):
            word = word | lax.shift_left(visible[b, column], g)
        words = jnp.where(lane == b, word, words)
    out_ref[0:3, :] = positions[...]
    out_ref[3:5, :] = reflectivity[...]
    out_ref[5:8, :LANES] = jnp.concatenate([row, words.astype(f32), jnp.zeros_like(row)], axis=0)
    out_ref[5:8, LANES:] = jnp.zeros((3, out_ref.shape[1] - LANES), f32)


def pack_facets(ids, positions, reflectivity, visible, groups, group_len):
    return pl.pallas_call(
        functools.partial(pack_kernel, groups, group_len),
        out_shape=jax.ShapeDtypeStruct((8, positions.shape[1]), f32),
        in_specs=[pl.BlockSpec(memory_space=pl.ANY)] * 4,
        out_specs=pl.BlockSpec(memory_space=pltpu.VMEM),
        scratch_shapes=[
            pltpu.SMEM(ids.shape, jnp.int32),
            pltpu.VMEM(positions.shape, f32),
            pltpu.VMEM(reflectivity.shape, f32),
            pltpu.SMEM(visible.shape, jnp.int32),
            pltpu.SemaphoreType.DMA((4,)),
        ],
        compiler_params=pltpu.CompilerParams(vmem_limit_bytes=ALL_VMEM),
        name="pack_facets",
    )(ids, positions, reflectivity, visible)


def transform_tables_kernel(
    facet_n, pulse_n, order, share, group_len, pulses, bins_dev, k_block,
    after_ref, w_ref, chirp_ref,
):
    mine_f, mine_z = lax.axis_index("facet"), lax.axis_index("pulse")
    k_ids = mine_f * k_block + lax.broadcasted_iota(jnp.int32, (k_block, LANES), 0)
    lane = lax.broadcasted_iota(jnp.int32, (k_block, LANES), 1)
    pulse_dev = pulses // pulse_n

    def rotation(index):
        back = (index + pulses // 2) % pulses - pulses // 2
        cosine, sine = cis_turns(back.astype(f32) * (1.0 / pulses))
        return cosine, -sine

    slot = lane // share
    within = lane % share
    here = (mine_z ^ (slot % pulse_n)) * pulse_dev + (
        within // group_len * facet_n + mine_f
    ) * group_len + within % group_len
    scale = 1.0 / math.sqrt(pulses)
    real, imag = rotation((k_ids * here) % pulses)
    wide = {0: (real * scale, imag * scale)}
    per_block = LANES // share
    turns = []
    bit = 1
    while bit < pulse_n:
        if bit >= per_block:
            sign = 1 - 2 * ((mine_z // bit) % 2)
            turns.append(sign * pulse_dev * bit)
        bit *= 2
    for bit in order:
        sign = 1 - 2 * ((mine_f // bit) % 2)
        turns.append(sign * group_len * bit)
    for level, turn in enumerate(turns):
        rr, ri = rotation((k_ids * turn) % pulses)
        for at in range(1 << level):
            real, imag = wide[at]
            wide[at + (1 << level)] = (real * rr - imag * ri, real * ri + imag * rr)
    for at, (real, imag) in wide.items():
        w_ref[:k_block, at * LANES : at * LANES + LANES] = real.astype(bf16)
        w_ref[k_block:, at * LANES : at * LANES + LANES] = imag.astype(bf16)
    offset = mine_f * k_block - pulses // 2 + lax.broadcasted_iota(jnp.int32, (k_block, bins_dev), 0)
    bins = mine_z * bins_dev + lax.broadcasted_iota(jnp.int32, (k_block, bins_dev), 1)
    phase = (offset * offset).astype(f32) * (8.0 / (2.0 * pulses)) / (8.0 + bins.astype(f32))
    cosine, sine = cis_turns(phase - jnp.round(phase))
    chirp_ref[0] = cosine
    chirp_ref[1] = sine


def transform_tables(after, facet_n, pulse_n, order, share, group_len, pulses, bins_dev, k_block):
    return pl.pallas_call(
        functools.partial(
            transform_tables_kernel, facet_n, pulse_n, order, share, group_len, pulses, bins_dev, k_block
        ),
        out_shape=(
            jax.ShapeDtypeStruct((2 * k_block, pulses), bf16),
            jax.ShapeDtypeStruct((2, k_block, bins_dev), f32),
        ),
        in_specs=[pl.BlockSpec(memory_space=pl.ANY)],
        out_specs=(pl.BlockSpec(memory_space=pltpu.VMEM),) * 2,
        compiler_params=pltpu.CompilerParams(vmem_limit_bytes=16 << 20),
        name="transform_tables",
    )(after)


def transform_kernel(k_block, bins_dev, w_ref, chirp_ref, *refs):
    pieces, out_ref = refs[:-1], refs[-1]
    total = None
    at = 0
    for piece in pieces:
        rows = piece.shape[0]
        part = jnp.dot(w_ref[:, at : at + rows], piece[...], preferred_element_type=f32)
        total = part if total is None else total + part
        at += rows
    real = total[:k_block, :bins_dev] - total[k_block:, bins_dev:]
    imag = total[k_block:, :bins_dev] + total[:k_block, bins_dev:]
    cosine, sine = chirp_ref[0], chirp_ref[1]
    out_ref[0] = (cosine * real - sine * imag).T
    out_ref[1] = (cosine * imag + sine * real).T


def transform(w, chirp, pieces, k_block, bins_dev):
    return pl.pallas_call(
        functools.partial(transform_kernel, k_block, bins_dev),
        out_shape=jax.ShapeDtypeStruct((2, bins_dev, k_block), f32),
        in_specs=[pl.BlockSpec(memory_space=pltpu.VMEM)] * (2 + len(pieces)),
        out_specs=pl.BlockSpec(memory_space=pltpu.VMEM),
        compiler_params=pltpu.CompilerParams(vmem_limit_bytes=16 << 20),
        name="transform",
    )(w, chirp, *pieces)


def swap(x, axis, size, mask):
    return lax.ppermute(x, axis, [(i, i ^ mask) for i in range(size)])


def gather_facet(x, size):
    near = [x] + [swap(x, "facet", size, mask) for mask in range(size - 2, 0, -2)]
    near = [near[0]] + near[:0:-1]
    out = []
    for piece in near:
        out += [piece, swap(piece, "facet", size, 1)]
    return out


def body(facet_positions, reflectivity, block_building, visible, platform):
    facet_n = lax.axis_size("facet")
    pulse_n = lax.axis_size("pulse")
    mine_z = lax.axis_index("pulse")
    pulse_dev = platform.shape[1]
    pulses = pulse_dev * pulse_n
    blocks = facet_positions.shape[1] // BLK
    share = pulse_dev // facet_n
    group_len = min(8, share)
    groups = share // group_len
    bins_dev = BINS // pulse_n
    k_block = pulses // facet_n
    buildings = visible.shape[0]

    packed = pack_facets(
        block_building, facet_positions, reflectivity, visible, groups, group_len
    )
    facets = gather_facet(packed, facet_n)

    mine_f = lax.axis_index("facet")
    facets[0] = packed * (mine_f >= 0).astype(f32)
    stations = platform * (1.0 / (16.0 * math.pi))
    one = (mine_f >= 0).astype(bf16)
    fold = jnp.broadcast_to(jnp.asarray(fold_matrix(), bf16)[:, None, :], (256, 8, 256)) * one
    fold = fold.reshape(2048, 256)

    echo = echoes(buildings, stations, fold, facets, blocks, groups, group_len)
    order = [1 << i for i in range(facet_n.bit_length() - 1)]
    w, chirp = transform_tables(
        echo, facet_n, pulse_n, order, share, group_len, pulses, bins_dev, k_block
    )

    echo = echo.reshape(QUADS, groups, 8, 2, LANES)[:, :, :group_len]
    if pulse_n > QUADS:
        echo = echo.reshape(QUADS, share, 2, pulse_n // QUADS, bins_dev).transpose(0, 3, 1, 2, 4)
    echo = echo.reshape(pulse_n, share, 2 * bins_dev)
    turned = [lax.dynamic_index_in_dim(echo, mine_z, 0, keepdims=False)]
    for mask in range(1, pulse_n):
        piece = lax.dynamic_index_in_dim(echo, mine_z ^ mask, 0, keepdims=False)
        turned.append(swap(piece, "pulse", pulse_n, mask))
    turned, w, chirp = lax.optimization_barrier((jnp.concatenate(turned), w, chirp))

    pieces = gather_facet(turned, facet_n)
    return transform(w, chirp, pieces, k_block, bins_dev)


def solution(mesh):
    placed = (P(None, "facet"), P(None, "facet"), P("facet"), P(None, "pulse"), P(None, "pulse"))
    return jax.shard_map(
        body, mesh=mesh, in_specs=placed, out_specs=P(None, "pulse", "facet"), check_vma=False
    )
```

```python
import functools
import math

import jax
import jax.numpy as jnp
import numpy as np
from jax import lax
from jax.experimental import pallas as pl
from jax.experimental.pallas import tpu as pltpu
from jax.sharding import PartitionSpec as P


BLK = 128
PBS = 32
BINS = 512
LANES = 128
STEP = 4
QUADS = 4


f32 = jnp.float32
bf16 = jnp.bfloat16

SIN_C = (4.442882878126042, -7.308239958462742, 3.606233657443361, -0.8453187380162854, 0.10822102663962477)
COS_C = (-1.4142135611352313, 6.978863916510845, -5.739875235214542, 1.8882041596407644, -0.33193097868538995, 0.03399741622323665)


def poly(coefs, w):
    acc = w * coefs[-1] + coefs[-2]
    for c in coefs[-3::-1]:
        acc = acc * w + c
    return acc


def cis_turns(v):
    w = v * v
    s = v * poly(SIN_C, w)
    c = poly(COS_C, w)
    return 1.0 - s * s, -(s * c)


def fold_matrix():
    left = np.zeros((8, 2, 4))
    for m in range(2):
        plus, minus = (2 + m, 1 - m)
        for which, (c, sign) in enumerate(((0, 1), (0, 1), (1, 1), (1, -1))):
            left[m * 4 + which, c, plus] = sign
            left[m * 4 + which, c, minus] = (sign, -sign)[which % 2]
    right = np.zeros((16, 2, 2, 16))
    for mp in range(2):
        for m in range(2):
            for low in range(2):
                middle, off = 4 + 8 * (2 * mp + low), (1, 3)[m]
                for which, (cs, plus, minus) in enumerate(((0, 1, 1), (0, -1, 1), (1, 1, 1), (1, 1, -1))):
                    right[mp * 8 + m * 4 + which, low, cs, (middle + off - 1) // 2] = plus
                    right[mp * 8 + m * 4 + which, low, cs, (middle - off - 1) // 2] = minus
    both = np.einsum("tca,ulsj->tulcsaj", left, right)
    out = np.zeros((8, 16, 2, 2, 4, 32))
    up, down = slice(16, 32), slice(15, None, -1)
    out[:, :, :, 0, :, up] = both[:, :, :, 0, 0] + both[:, :, :, 1, 1]
    out[:, :, :, 0, :, down] = both[:, :, :, 0, 0] - both[:, :, :, 1, 1]
    out[:, :, :, 1, :, up] = both[:, :, :, 1, 0] - both[:, :, :, 0, 1]
    out[:, :, :, 1, :, down] = both[:, :, :, 1, 0] + both[:, :, :, 0, 1]
    return out.reshape(8 * 32, 2 * 4 * 32) / 16.0


def pack(low, high):
    return jnp.concatenate([low, high], axis=0).astype(bf16)


def block_angles(x, y, z, ax, ay, az):
    dx, dy, dz = x - ax, y - ay, z - az
    d2 = dx * dx + dy * dy + dz * dz
    t = d2 * lax.rsqrt(d2) - 1.25
    w = t * t
    s = t * poly(SIN_C, w)
    return s * poly(COS_C, w), 1.0 - s * s


def block_factors(c1, s1, r0, r1):
    square = c1 * c1
    a2, b2 = 4.0 * square - 2.0, 4.0 * (c1 * s1)
    c3, s3 = (a2 - 1.0) * c1, (a2 + 1.0) * s1
    a4, b4 = a2 * a2 - 2.0, a2 * b2
    a8, b8 = a4 * a4 - 2.0, a4 * b4
    a12, b12 = (a8 - 1.0) * a4, (a8 + 1.0) * b4
    a20, b20 = a8 * a12 - a4, a8 * b12 - b4
    a28, b28 = a8 * a20 - a12, a8 * b20 - b12
    a16, b16 = a8 * a8 - 2.0, a8 * b8
    a32, b32 = a16 * a16 - 2.0, a16 * b16
    a64, b64 = a32 * a32 - 2.0, a32 * b32
    a128, b128 = a64 * a64 - 2.0, a64 * b64
    a256, b256 = a128 * a128 - 2.0, a128 * b128
    a96, b96 = (a64 - 1.0) * a32, (a64 + 1.0) * b32
    c256, s256 = 0.5 * a256, 0.5 * b256
    c144, s144 = a128 * a16 - b128 * b16, b128 * a16 + a128 * b16
    c143, s143 = c144 * c1 + s144 * s1, s144 * c1 - c144 * s1
    q0r, q0i = r0 * c143 + r1 * s143, r1 * c143 - r0 * s143
    q1r, q1i = q0r * c256 + q0i * s256, q0i * c256 - q0r * s256
    q2r, q2i = a256 * q1r - q0r, a256 * q1i - q0i
    q3r, q3i = a256 * q2r - q1r, a256 * q2i - q1i
    return (
        a32, b32, a96, b96, q0r, q0i, q1r, q1i, q2r, q2i, q3r, q3i,
        c1, s1, c3, s3, a4, b4, a12, b12, a20, b20, a28, b28,
    )


def table_of(factors):
    near, far = factors[:4], factors[4:]
    near = [pack(value, value) for value in near]
    tiles = []
    for low in (0, 4):
        real, imag = pack(far[low], far[low + 2]), pack(far[low + 1], far[low + 3])
        for cosine, sine in (near[0:2], near[2:4]):
            tiles += [real * cosine, imag * sine, imag * cosine, real * sine]
    return jnp.concatenate(tiles, axis=0)


def echo_kernel(
    pieces, blocks, groups, group_len, buildings,
    platform_ref, fold, *refs,
):
    piece_refs = refs[:pieces]
    out_ref, fac_ref, marks_v, marks_s, rows_s, antenna, angles, products, sem = refs[pieces:]
    mine = lax.axis_index("facet")
    in_turns = 1.0 / (16.0 * math.pi)
    scale = jnp.where(lax.broadcasted_iota(jnp.int32, (8, LANES), 0) < 3, in_turns, 1.0)
    for piece, ref in enumerate(piece_refs):
        for j in range(blocks):
            at = (piece * blocks + j) * 8
            fac_ref[at : at + 8, :] = ref[:, j * LANES : j * LANES + LANES] * scale
    fac_ref[pieces * blocks * 8 :, :] = jnp.zeros((8, LANES), f32)
    ids = jnp.concatenate([ref[5:6, :LANES] for ref in piece_refs], axis=0)
    marks = jnp.zeros(ids.shape, jnp.int32)
    for b in range(buildings):
        marks = jnp.where(ids == float(b), piece_refs[0][6:7, b : b + 1].astype(jnp.int32), marks)
    marks_v[:pieces, :] = marks
    marks_v[pieces:, :] = jnp.zeros((8, LANES), jnp.int32)
    marks_copy = pltpu.make_async_copy(marks_v, marks_s, sem)
    marks_copy.start()
    pulse_dev = platform_ref.shape[1]
    flat = platform_ref[...] * in_turns
    flat = jnp.concatenate([flat, jnp.zeros((8 - flat.shape[0], pulse_dev), f32)], axis=0)
    antenna[:pulse_dev, :8] = flat.T
    antenna[pulse_dev:, :] = jnp.zeros((8, LANES), f32)
    marks_copy.wait()
    most = pieces * blocks + 3 * STEP

    def scan(piece, g, at):
        for j in range(blocks):
            rows_s[at] = (piece * blocks + j) * 8
            at = at + (lax.shift_right_logical(marks_s[piece, j], g) & 1)
        return at

    def close(at):
        for extra in range(3 * STEP):
            rows_s[at + extra] = pieces * blocks * 8

    def station(g):
        g = jnp.minimum(g, groups - 1)
        ant = antenna[pl.ds((g * pieces + mine) * group_len, 8), :]
        return [jnp.broadcast_to(ant[:, i : i + 1], (8, LANES)) for i in range(3)]

    def turn(at, place):
        for j in range(STEP):
            row = rows_s[at + j]
            facet = [fac_ref[pl.ds(row + c, 8, stride=0), :] for c in range(3)]
            angles[j, 0], angles[j, 1] = block_angles(*facet, *place)

    def read(at, j):
        row = rows_s[at + j]
        weights = [fac_ref[pl.ds(row + c, 8, stride=0), :] for c in (3, 4)]
        return angles[j, 0], angles[j, 1], *weights

    same = (
        lax.broadcasted_iota(jnp.int32, (16, 256), 0) % 8
        == lax.broadcasted_iota(jnp.int32, (16, 256), 1) % 8
    )

    def group(acc0, acc1, g, count):
        place = station(g)
        here, there = (g % 2) * most, ((g + 1) % 2) * most
        steps = jnp.maximum(lax.div(count + (STEP - 1), STEP), 1)

        def step(i, at):
            for half, acc in ((0, acc0), (1, acc1)):
                pair = [block_factors(*read(here + i * STEP, 2 * half + j)) for j in range(2)]
                right = jnp.concatenate([table_of(p[12:]) for p in pair], axis=1)
                left = jnp.concatenate([table_of(p[:12]) for p in pair], axis=1)
                pltpu.matmul_push_rhs(right, staging_register=0, mxu_index=half, transpose=True)
                pltpu.matmul_acc_lhs(acc, left, load_staged_rhs=0)
            turn(here + (i + 1) * STEP, place)
            return scan(jnp.minimum(i, pieces), g + 1, at)

        at = lax.fori_loop(0, steps, step, there)
        at = lax.fori_loop(
            jnp.minimum(steps, pieces), pieces, lambda piece, n: scan(piece, g + 1, n), at
        )
        close(at)
        turn(there, station(g + 1))
        total = pltpu.matmul_pop(acc0) + pltpu.matmul_pop(acc1)
        for tile in range(16):
            hp, spot = tile // 8, tile % 8
            kept = jnp.where(same, total[tile * 16 : tile * 16 + 16, :], 0.0).astype(bf16)
            products[hp, pl.ds(pl.multiple_of(g * 16, 16), 16), spot * 256 : spot * 256 + 256] = kept
        return at - there

    first = lax.fori_loop(0, pieces, lambda piece, n: scan(piece, 0, n), jnp.int32(0))
    close(first)
    turn(0, station(0))
    pl.run_scoped(
        lambda acc0, acc1: lax.fori_loop(0, groups, functools.partial(group, acc0, acc1), first),
        pltpu.ACC(0)((256, 256), f32), pltpu.ACC(1)((256, 256), f32),
    )
    pl.run_scoped(
        functools.partial(fold_products, groups, products, fold, out_ref),
        pltpu.ACC(0)((groups * 16, 256), f32), pltpu.ACC(1)((groups * 16, 256), f32),
    )


def fold_products(groups, products, fold, out_ref, *accs):
    for k in range(8):
        lanes = slice(k * 256, k * 256 + 256)
        for hp, acc in enumerate(accs):
            pltpu.matmul_push_rhs(fold[lanes, :], staging_register=k % 2, mxu_index=hp)
            pltpu.matmul_acc_lhs(acc, products[hp, :, lanes], load_staged_rhs=k % 2)
    for hp, acc in enumerate(accs):
        echo = pltpu.matmul_pop(acc)
        for low in range(2):
            picked = [echo[g * 16 + low * 8 : g * 16 + low * 8 + 8] for g in range(groups)]
            out_ref[2 * hp + low] = jnp.concatenate(picked, axis=0).astype(bf16)


def echoes(buildings, platform, fold, facets, blocks, groups, group_len):
    pieces = len(facets)
    most = pieces * blocks + 3 * STEP
    pulse_dev = platform.shape[1]
    vmem = pl.BlockSpec(memory_space=pltpu.VMEM)
    return pl.pallas_call(
        functools.partial(echo_kernel, pieces, blocks, groups, group_len, buildings),
        out_shape=jax.ShapeDtypeStruct((QUADS, groups * 8, 256), bf16),
        in_specs=[vmem] * (2 + pieces),
        out_specs=vmem,
        scratch_shapes=[
            pltpu.VMEM(((pieces * blocks + 1) * 8, LANES), f32),
            pltpu.VMEM((pieces + 8, LANES), jnp.int32),
            pltpu.SMEM((pieces + 8, LANES), jnp.int32),
            pltpu.SMEM((2 * most + 3 * STEP,), jnp.int32),
            pltpu.VMEM((pulse_dev + 8, LANES), f32),
            pltpu.VMEM((STEP, 2, 8, LANES), f32),
            pltpu.VMEM((2, groups * 16, 2048), bf16),
            pltpu.SemaphoreType.DMA,
        ],
        compiler_params=pltpu.CompilerParams(vmem_limit_bytes=16 << 20),
        name="echoes",
    )(platform, fold, *facets)


def pack_kernel(
    groups, group_len, ids_hbm, positions_hbm, reflectivity_hbm, visible_hbm, platform_hbm,
    out_ref, stations_ref, ids, positions, reflectivity, visible, sems,
):
    mine, count = lax.axis_index("facet"), lax.axis_size("facet")
    copies = [
        pltpu.make_async_copy(source, target, sems.at[i])
        for i, (source, target) in enumerate((
            (visible_hbm, visible), (ids_hbm, ids),
            (positions_hbm, positions), (reflectivity_hbm, reflectivity), (platform_hbm, stations_ref),
        ))
    ]
    for copy in copies:
        copy.start()
    for copy in copies[:2]:
        copy.wait()
    lane = lax.broadcasted_iota(jnp.int32, (1, LANES), 1)
    row = jnp.zeros(lane.shape, f32)
    for j in range(ids.shape[0]):
        row = jnp.where(lane == j, ids[j].astype(f32), row)
    words = jnp.zeros(lane.shape, jnp.int32)
    columns = [lax.div((g * count + mine) * group_len, PBS) for g in range(groups)]
    for b in range(visible.shape[0]):
        word = jnp.int32(0)
        for g, column in enumerate(columns):
            word = word | lax.shift_left(visible[b, column], g)
        words = jnp.where(lane == b, word, words)
    for copy in copies[2:]:
        copy.wait()
    out_ref[0:3, :] = positions[...]
    out_ref[3:5, :] = reflectivity[...]
    out_ref[5:8, :LANES] = jnp.concatenate([row, words.astype(f32), jnp.zeros_like(row)], axis=0)
    out_ref[5:8, LANES:] = jnp.zeros((3, out_ref.shape[1] - LANES), f32)


def in_hbm(x):
    return pltpu.with_memory_space_constraint(x, pltpu.HBM)


def pack_facets(ids, positions, reflectivity, visible, platform, groups, group_len):
    vmem = pl.BlockSpec(memory_space=pltpu.VMEM)
    return pl.pallas_call(
        functools.partial(pack_kernel, groups, group_len),
        out_shape=(
            jax.ShapeDtypeStruct((8, positions.shape[1]), f32),
            jax.ShapeDtypeStruct(platform.shape, f32),
        ),
        in_specs=[pl.BlockSpec(memory_space=pltpu.HBM)] * 5,
        out_specs=(vmem, vmem),
        scratch_shapes=[
            pltpu.SMEM(ids.shape, jnp.int32),
            pltpu.VMEM(positions.shape, f32),
            pltpu.VMEM(reflectivity.shape, f32),
            pltpu.SMEM(visible.shape, jnp.int32),
            pltpu.SemaphoreType.DMA((5,)),
        ],
        compiler_params=pltpu.CompilerParams(vmem_limit_bytes=4 << 20),
        name="pack_facets",
    )(*map(in_hbm, (ids, positions, reflectivity, visible, platform)))


def transform_tables_kernel(
    facet_n, pulse_n, order, share, group_len, pulses, bins_dev, k_block,
    after_ref, w_ref, chirp_ref,
):
    mine_f, mine_z = lax.axis_index("facet"), lax.axis_index("pulse")
    k_ids = mine_f * k_block + lax.broadcasted_iota(jnp.int32, (k_block, LANES), 0)
    lane = lax.broadcasted_iota(jnp.int32, (k_block, LANES), 1)
    pulse_dev = pulses // pulse_n

    def rotation(index):
        back = (index + pulses // 2) % pulses - pulses // 2
        cosine, sine = cis_turns(back.astype(f32) * (1.0 / pulses))
        return cosine, -sine

    slot = lane // share
    within = lane % share
    here = (mine_z ^ (slot % pulse_n)) * pulse_dev + (
        within // group_len * facet_n + mine_f
    ) * group_len + within % group_len
    scale = 1.0 / math.sqrt(pulses)
    real, imag = rotation((k_ids * here) % pulses)
    wide = {0: (real * scale, imag * scale)}
    per_block = LANES // share
    turns = []
    bit = 1
    while bit < pulse_n:
        if bit >= per_block:
            sign = 1 - 2 * ((mine_z // bit) % 2)
            turns.append(sign * pulse_dev * bit)
        bit *= 2
    for bit in order:
        sign = 1 - 2 * ((mine_f // bit) % 2)
        turns.append(sign * group_len * bit)
    for level, turn in enumerate(turns):
        rr, ri = rotation((k_ids * turn) % pulses)
        for at in range(1 << level):
            real, imag = wide[at]
            wide[at + (1 << level)] = (real * rr - imag * ri, real * ri + imag * rr)
    for at, (real, imag) in wide.items():
        w_ref[:k_block, at * LANES : at * LANES + LANES] = real.astype(bf16)
        w_ref[k_block:, at * LANES : at * LANES + LANES] = imag.astype(bf16)
    offset = mine_f * k_block - pulses // 2 + lax.broadcasted_iota(jnp.int32, (k_block, bins_dev), 0)
    bins = mine_z * bins_dev + lax.broadcasted_iota(jnp.int32, (k_block, bins_dev), 1)
    phase = (offset * offset).astype(f32) * (8.0 / (2.0 * pulses)) / (8.0 + bins.astype(f32))
    cosine, sine = cis_turns(phase - jnp.round(phase))
    chirp_ref[0] = cosine
    chirp_ref[1] = sine


def transform_tables(after, facet_n, pulse_n, order, share, group_len, pulses, bins_dev, k_block):
    return pl.pallas_call(
        functools.partial(
            transform_tables_kernel, facet_n, pulse_n, order, share, group_len, pulses, bins_dev, k_block
        ),
        out_shape=(
            jax.ShapeDtypeStruct((2 * k_block, pulses), bf16),
            jax.ShapeDtypeStruct((2, k_block, bins_dev), f32),
        ),
        in_specs=[pl.BlockSpec(memory_space=pl.ANY)],
        out_specs=(pl.BlockSpec(memory_space=pltpu.VMEM),) * 2,
        compiler_params=pltpu.CompilerParams(vmem_limit_bytes=16 << 20),
        name="transform_tables",
    )(after)


def transform_kernel(places, has_total, k_block, bins_dev, w_ref, *refs):
    total = refs[0][...] if has_total else None
    pieces = refs[has_total : has_total + len(places)]
    for place, piece in zip(places, pieces):
        rows = piece.shape[0]
        part = jnp.dot(
            w_ref[:, place * rows : place * rows + rows], piece[...], preferred_element_type=f32
        )
        total = part if total is None else total + part
    rest = refs[has_total + len(places) :]
    if len(rest) == 1:
        rest[0][...] = total
        return
    chirp_ref, out_ref = rest
    real = total[:k_block, :bins_dev] - total[k_block:, bins_dev:]
    imag = total[k_block:, :bins_dev] + total[:k_block, bins_dev:]
    cosine, sine = chirp_ref[0], chirp_ref[1]
    out_ref[0] = (cosine * real - sine * imag).T
    out_ref[1] = (cosine * imag + sine * real).T


def transform(w, total, pieces, places, k_block, bins_dev, chirp=None):
    operands = [w] + ([] if total is None else [total]) + [pieces[at] for at in places]
    shape = (2 * k_block, 2 * bins_dev)
    if chirp is not None:
        operands.append(chirp)
        shape = (2, bins_dev, k_block)
    vmem = pl.BlockSpec(memory_space=pltpu.VMEM)
    return pl.pallas_call(
        functools.partial(transform_kernel, places, total is not None, k_block, bins_dev),
        out_shape=jax.ShapeDtypeStruct(shape, f32),
        in_specs=[vmem] * len(operands),
        out_specs=vmem,
        compiler_params=pltpu.CompilerParams(vmem_limit_bytes=16 << 20),
        name="transform",
    )(*operands)


def swap(x, axis, size, mask):
    return lax.ppermute(x, axis, [(i, i ^ mask) for i in range(size)])


def gather_facet(x, size):
    near = [x]
    for mask in range(2, size, 2):
        near.append(swap(x, "facet", size, mask))
    out = []
    for mask, piece in zip(range(0, size, 2), near):
        out += [piece, swap(piece, "facet", size, 1)]
    return out


def body(facet_positions, reflectivity, block_building, visible, platform):
    facet_n = lax.axis_size("facet")
    pulse_n = lax.axis_size("pulse")
    mine_z = lax.axis_index("pulse")
    pulse_dev = platform.shape[1]
    pulses = pulse_dev * pulse_n
    blocks = facet_positions.shape[1] // BLK
    share = pulse_dev // facet_n
    group_len = min(8, share)
    groups = share // group_len
    bins_dev = BINS // pulse_n
    k_block = pulses // facet_n
    buildings = visible.shape[0]

    packed, stations = pack_facets(
        block_building, facet_positions, reflectivity, visible, platform, groups, group_len
    )
    facets = gather_facet(packed, facet_n)

    one = (lax.axis_index("facet") >= 0).astype(bf16)
    fold = jnp.broadcast_to(jnp.asarray(fold_matrix(), bf16)[:, None, :], (256, 8, 256)) * one
    fold = fold.reshape(2048, 256)
    echo = echoes(buildings, stations, fold, facets, blocks, groups, group_len)
    order = [1 << i for i in range(facet_n.bit_length() - 1)]
    w, chirp = transform_tables(
        echo, facet_n, pulse_n, order, share, group_len, pulses, bins_dev, k_block
    )

    echo = echo.reshape(QUADS, groups, 8, 2, LANES)[:, :, :group_len]
    if pulse_n > QUADS:
        echo = echo.reshape(QUADS, share, 2, pulse_n // QUADS, bins_dev).transpose(0, 3, 1, 2, 4)
    echo = echo.reshape(pulse_n, share, 2 * bins_dev)
    turned = [lax.dynamic_index_in_dim(echo, mine_z, 0, keepdims=False)]
    for mask in range(1, pulse_n):
        piece = lax.dynamic_index_in_dim(echo, mine_z ^ mask, 0, keepdims=False)
        turned.append(swap(piece, "pulse", pulse_n, mask))
    turned, w, chirp = lax.optimization_barrier((jnp.concatenate(turned), w, chirp))

    pieces = gather_facet(turned, facet_n)
    total = transform(w, None, pieces, [0, 1], k_block, bins_dev)
    total = transform(w, total, pieces, list(range(2, facet_n, 2)), k_block, bins_dev)
    return transform(w, total, pieces, list(range(3, facet_n, 2)), k_block, bins_dev, chirp)


def solution(mesh):
    placed = (P(None, "facet"), P(None, "facet"), P("facet"), P(None, "pulse"), P(None, "pulse"))
    return jax.shard_map(body, mesh=mesh, in_specs=placed, out_specs=P(None, "pulse", "facet"), check_vma=False)
```

```python
import functools
import math

import jax
import jax.numpy as jnp
import numpy as np
from jax import lax
from jax.experimental import pallas as pl
from jax.experimental.pallas import tpu as pltpu
from jax.sharding import PartitionSpec as P


BLK = 128
PBS = 32
BINS = 512
LANES = 128
WIDE = 8
NARROW = 4
QUADS = 4


f32 = jnp.float32
bf16 = jnp.bfloat16

SIN_C = (4.442882878126042, -7.308239958462742, 3.606233657443361, -0.8453187380162854, 0.10822102663962477)
COS_C = (-1.4142135611352313, 6.978863916510845, -5.739875235214542, 1.8882041596407644, -0.33193097868538995, 0.03399741622323665)


def poly(coefs, w):
    acc = w * coefs[-1] + coefs[-2]
    for c in coefs[-3::-1]:
        acc = acc * w + c
    return acc


def cis_turns(v):
    w = v * v
    s = v * poly(SIN_C, w)
    c = poly(COS_C, w)
    return 1.0 - s * s, -(s * c)


def fold_matrix():
    left = np.zeros((8, 2, 4))
    for m in range(2):
        plus, minus = (2 + m, 1 - m)
        for which, (c, sign) in enumerate(((0, 1), (0, 1), (1, 1), (1, -1))):
            left[m * 4 + which, c, plus] = sign
            left[m * 4 + which, c, minus] = (sign, -sign)[which % 2]
    right = np.zeros((16, 2, 2, 16))
    for f16, ff, m, fn in np.ndindex(2, 2, 2, 2):
        for low in range(2):
            for e, d in ((1, 1), (1, -1), (-1, 1), (-1, -1)):
                far, near = (4, 12)[low], (1, 3)[m]
                sines = f16 + ff + fn
                value = (e if ff else 1) * (d if fn else 1) * (-1) ** (sines // 2)
                right[f16 * 8 + ff * 4 + m * 2 + fn, low, sines % 2, (15 + e * far + d * near) // 2] = value
    both = np.einsum("tca,ulsj->tulcsaj", left, right)
    out = np.zeros((8, 16, 2, 2, 4, 32))
    up, down = slice(16, 32), slice(15, None, -1)
    out[:, :, :, 0, :, up] = both[:, :, :, 0, 0] + both[:, :, :, 1, 1]
    out[:, :, :, 0, :, down] = both[:, :, :, 0, 0] - both[:, :, :, 1, 1]
    out[:, :, :, 1, :, up] = both[:, :, :, 1, 0] - both[:, :, :, 0, 1]
    out[:, :, :, 1, :, down] = both[:, :, :, 1, 0] + both[:, :, :, 0, 1]
    return out.reshape(8 * 32, 2 * 4 * 32) / 32.0


def pack(low, high):
    return jnp.concatenate([low, high], axis=0).astype(bf16)


def block_angles(x, y, z, ax, ay, az):
    dx, dy, dz = x - ax, y - ay, z - az
    d2 = dx * dx + dy * dy + dz * dz
    t = d2 * lax.rsqrt(d2) - 1.25
    w = t * t
    s = t * poly(SIN_C, w)
    return s * poly(COS_C, w), 1.0 - s * s


def block_factors(c1, s1, r0, r1):
    square = c1 * c1
    a2, b2 = 4.0 * square - 2.0, 4.0 * (c1 * s1)
    c3, s3 = (a2 - 1.0) * c1, (a2 + 1.0) * s1
    a4, b4 = a2 * a2 - 2.0, a2 * b2
    a8, b8 = a4 * a4 - 2.0, a4 * b4
    a12, b12 = (a8 - 1.0) * a4, (a8 + 1.0) * b4
    a16, b16 = a8 * a8 - 2.0, a8 * b8
    a32, b32 = a16 * a16 - 2.0, a16 * b16
    a64, b64 = a32 * a32 - 2.0, a32 * b32
    a128, b128 = a64 * a64 - 2.0, a64 * b64
    a256, b256 = a128 * a128 - 2.0, a128 * b128
    a96, b96 = (a64 - 1.0) * a32, (a64 + 1.0) * b32
    c256, s256 = 0.5 * a256, 0.5 * b256
    c144, s144 = a128 * a16 - b128 * b16, b128 * a16 + a128 * b16
    c143, s143 = c144 * c1 + s144 * s1, s144 * c1 - c144 * s1
    q0r, q0i = r0 * c143 + r1 * s143, r1 * c143 - r0 * s143
    q1r, q1i = q0r * c256 + q0i * s256, q0i * c256 - q0r * s256
    q2r, q2i = a256 * q1r - q0r, a256 * q1i - q0i
    q3r, q3i = a256 * q2r - q1r, a256 * q2i - q1i
    return (
        a32, b32, a96, b96, q0r, q0i, q1r, q1i, q2r, q2i, q3r, q3i,
        a16, b16, a4, b4, a12, b12, c1, s1, c3, s3,
    )


def left_table(factors):
    near = [pack(value, value) for value in factors[:4]]
    far = factors[4:]
    tiles = []
    for low in (0, 4):
        real, imag = pack(far[low], far[low + 2]), pack(far[low + 1], far[low + 3])
        for cosine, sine in (near[0:2], near[2:4]):
            tiles += [real * cosine, imag * sine, imag * cosine, real * sine]
    return jnp.concatenate(tiles, axis=0)


def right_table(factors):
    middle = [pack(value, value) for value in factors[:2]]
    far = [pack(factors[2], factors[4]), pack(factors[3], factors[5])]
    near = [pack(value, value) for value in factors[6:]]
    return jnp.concatenate([(m * f) * n for m in middle for f in far for n in near], axis=0)


def echo_kernel(
    pieces, blocks, groups, group_len, buildings,
    platform_ref, fold, *refs,
):
    piece_refs = refs[:pieces]
    out_ref, fac_ref, marks_v, marks_s, rows_s, antenna, angles, products, sem = refs[pieces:]
    mine = lax.axis_index("facet")
    in_turns = 1.0 / (16.0 * math.pi)
    scale = jnp.where(lax.broadcasted_iota(jnp.int32, (8, LANES), 0) < 3, in_turns, 1.0)
    for piece, ref in enumerate(piece_refs):
        for j in range(blocks):
            at = (piece * blocks + j) * 8
            fac_ref[at : at + 8, :] = ref[:, j * LANES : j * LANES + LANES] * scale
    fac_ref[pieces * blocks * 8 :, :] = jnp.zeros((8, LANES), f32)
    ids = jnp.concatenate([ref[5:6, :LANES] for ref in piece_refs], axis=0)
    marks = jnp.zeros(ids.shape, jnp.int32)
    for b in range(buildings):
        marks = jnp.where(ids == float(b), piece_refs[0][6:7, b : b + 1].astype(jnp.int32), marks)
    marks_v[:pieces, :] = marks
    marks_v[pieces:, :] = jnp.zeros((8, LANES), jnp.int32)
    marks_copy = pltpu.make_async_copy(marks_v, marks_s, sem)
    marks_copy.start()
    pulse_dev = platform_ref.shape[1]
    flat = platform_ref[...] * in_turns
    flat = jnp.concatenate([flat, jnp.zeros((8 - flat.shape[0], pulse_dev), f32)], axis=0)
    antenna[:pulse_dev, :8] = flat.T
    antenna[pulse_dev:, :] = jnp.zeros((8, LANES), f32)
    marks_copy.wait()
    most = pieces * blocks + 2 * WIDE

    def scan(piece, g, at):
        for j in range(blocks):
            rows_s[at] = (piece * blocks + j) * 8
            at = at + (lax.shift_right_logical(marks_s[piece, j], g) & 1)
        return at

    def close(at):
        for extra in range(2 * WIDE):
            rows_s[at + extra] = pieces * blocks * 8

    def station(g):
        g = jnp.minimum(g, groups - 1)
        ant = antenna[pl.ds((g * pieces + mine) * group_len, 8), :]
        return [jnp.broadcast_to(ant[:, i : i + 1], (8, LANES)) for i in range(3)]

    def turn(at, place):
        for j in range(WIDE):
            row = rows_s[at + j]
            facet = [fac_ref[pl.ds(row + c, 8, stride=0), :] for c in range(3)]
            angles[j, 0], angles[j, 1] = block_angles(*facet, *place)

    def read(at, slot, j):
        row = rows_s[at + j]
        weights = [fac_ref[pl.ds(row + c, 8, stride=0), :] for c in (3, 4)]
        return angles[slot + j, 0], angles[slot + j, 1], *weights

    same = (
        lax.broadcasted_iota(jnp.int32, (16, 256), 0) % 8
        == lax.broadcasted_iota(jnp.int32, (16, 256), 1) % 8
    )

    def group(acc0, acc1, g, count):
        place = station(g)
        here, there = (g % 2) * most, ((g + 1) % 2) * most
        wide = lax.div(count, WIDE)
        narrow = lax.div(count - wide * WIDE + (NARROW - 1), NARROW)
        narrow = jnp.maximum(narrow, 1 - wide)

        def multiply(at, slot, blocks_here):
            for half in range(blocks_here // 2):
                pair = [block_factors(*read(at, slot, 2 * half + j)) for j in range(2)]
                right = jnp.concatenate([right_table(p[12:]) for p in pair], axis=1)
                left = jnp.concatenate([left_table(p[:12]) for p in pair], axis=1)
                unit, register = half % 2, half // 2
                pltpu.matmul_push_rhs(right, staging_register=register, mxu_index=unit, transpose=True)
                pltpu.matmul_acc_lhs((acc0, acc1)[unit], left, load_staged_rhs=register)

        def wide_step(i, at):
            multiply(here + i * WIDE, 0, WIDE)
            turn(here + (i + 1) * WIDE, place)
            at = scan(jnp.minimum(2 * i, pieces), g + 1, at)
            return scan(jnp.minimum(2 * i + 1, pieces), g + 1, at)

        def narrow_step(i, at):
            multiply(here + wide * WIDE + i * NARROW, i * NARROW, NARROW)
            return scan(jnp.minimum(2 * wide + i, pieces), g + 1, at)

        at = lax.fori_loop(0, wide, wide_step, there)
        at = lax.fori_loop(0, narrow, narrow_step, at)
        at = lax.fori_loop(
            jnp.minimum(2 * wide + narrow, pieces), pieces, lambda piece, n: scan(piece, g + 1, n), at
        )
        close(at)
        turn(there, station(g + 1))
        total = pltpu.matmul_pop(acc0) + pltpu.matmul_pop(acc1)
        for tile in range(16):
            hp, spot = tile // 8, tile % 8
            kept = jnp.where(same, total[tile * 16 : tile * 16 + 16, :], 0.0).astype(bf16)
            products[hp, pl.ds(pl.multiple_of(g * 16, 16), 16), spot * 256 : spot * 256 + 256] = kept
        return at - there

    first = lax.fori_loop(0, pieces, lambda piece, n: scan(piece, 0, n), jnp.int32(0))
    close(first)
    turn(0, station(0))
    pl.run_scoped(
        lambda acc0, acc1: lax.fori_loop(0, groups, functools.partial(group, acc0, acc1), first),
        pltpu.ACC(0)((256, 256), f32), pltpu.ACC(1)((256, 256), f32),
    )
    pl.run_scoped(
        functools.partial(fold_products, groups, products, fold, out_ref),
        pltpu.ACC(0)((groups * 16, 256), f32), pltpu.ACC(1)((groups * 16, 256), f32),
    )


def fold_products(groups, products, fold, out_ref, *accs):
    for k in range(8):
        lanes = slice(k * 256, k * 256 + 256)
        for hp, acc in enumerate(accs):
            pltpu.matmul_push_rhs(fold[lanes, :], staging_register=k % 2, mxu_index=hp)
            pltpu.matmul_acc_lhs(acc, products[hp, :, lanes], load_staged_rhs=k % 2)
    for hp, acc in enumerate(accs):
        echo = pltpu.matmul_pop(acc)
        for low in range(2):
            picked = [echo[g * 16 + low * 8 : g * 16 + low * 8 + 8] for g in range(groups)]
            out_ref[2 * hp + low] = jnp.concatenate(picked, axis=0).astype(bf16)


def echoes(buildings, platform, fold, facets, blocks, groups, group_len):
    pieces = len(facets)
    most = pieces * blocks + 2 * WIDE
    pulse_dev = platform.shape[1]
    vmem = pl.BlockSpec(memory_space=pltpu.VMEM)
    return pl.pallas_call(
        functools.partial(echo_kernel, pieces, blocks, groups, group_len, buildings),
        out_shape=jax.ShapeDtypeStruct((QUADS, groups * 8, 256), bf16),
        in_specs=[vmem] * (2 + pieces),
        out_specs=vmem,
        scratch_shapes=[
            pltpu.VMEM(((pieces * blocks + 1) * 8, LANES), f32),
            pltpu.VMEM((pieces + 8, LANES), jnp.int32),
            pltpu.SMEM((pieces + 8, LANES), jnp.int32),
            pltpu.SMEM((2 * most + 2 * WIDE,), jnp.int32),
            pltpu.VMEM((pulse_dev + 8, LANES), f32),
            pltpu.VMEM((WIDE, 2, 8, LANES), f32),
            pltpu.VMEM((2, groups * 16, 2048), bf16),
            pltpu.SemaphoreType.DMA,
        ],
        compiler_params=pltpu.CompilerParams(vmem_limit_bytes=16 << 20),
        name="echoes",
    )(platform, fold, *facets)


def pack_kernel(
    groups, group_len, ids_hbm, positions_hbm, reflectivity_hbm, visible_hbm, platform_hbm,
    out_ref, stations_ref, ids, positions, reflectivity, visible, sems,
):
    mine, count = lax.axis_index("facet"), lax.axis_size("facet")
    copies = [
        pltpu.make_async_copy(source, target, sems.at[i])
        for i, (source, target) in enumerate((
            (visible_hbm, visible), (ids_hbm, ids),
            (positions_hbm, positions), (reflectivity_hbm, reflectivity), (platform_hbm, stations_ref),
        ))
    ]
    for copy in copies:
        copy.start()
    for copy in copies[:2]:
        copy.wait()
    lane = lax.broadcasted_iota(jnp.int32, (1, LANES), 1)
    row = jnp.zeros(lane.shape, f32)
    for j in range(ids.shape[0]):
        row = jnp.where(lane == j, ids[j].astype(f32), row)
    words = jnp.zeros(lane.shape, jnp.int32)
    columns = [lax.div((g * count + mine) * group_len, PBS) for g in range(groups)]
    for b in range(visible.shape[0]):
        word = jnp.int32(0)
        for g, column in enumerate(columns):
            word = word | lax.shift_left(visible[b, column], g)
        words = jnp.where(lane == b, word, words)
    for copy in copies[2:]:
        copy.wait()
    out_ref[0:3, :] = positions[...]
    out_ref[3:5, :] = reflectivity[...]
    out_ref[5:8, :LANES] = jnp.concatenate([row, words.astype(f32), jnp.zeros_like(row)], axis=0)
    out_ref[5:8, LANES:] = jnp.zeros((3, out_ref.shape[1] - LANES), f32)


def in_hbm(x):
    return pltpu.with_memory_space_constraint(x, pltpu.HBM)


def pack_facets(ids, positions, reflectivity, visible, platform, groups, group_len):
    vmem = pl.BlockSpec(memory_space=pltpu.VMEM)
    return pl.pallas_call(
        functools.partial(pack_kernel, groups, group_len),
        out_shape=(
            jax.ShapeDtypeStruct((8, positions.shape[1]), f32),
            jax.ShapeDtypeStruct(platform.shape, f32),
        ),
        in_specs=[pl.BlockSpec(memory_space=pltpu.HBM)] * 5,
        out_specs=(vmem, vmem),
        scratch_shapes=[
            pltpu.SMEM(ids.shape, jnp.int32),
            pltpu.VMEM(positions.shape, f32),
            pltpu.VMEM(reflectivity.shape, f32),
            pltpu.SMEM(visible.shape, jnp.int32),
            pltpu.SemaphoreType.DMA((5,)),
        ],
        compiler_params=pltpu.CompilerParams(vmem_limit_bytes=4 << 20),
        name="pack_facets",
    )(*map(in_hbm, (ids, positions, reflectivity, visible, platform)))


def transform_tables_kernel(
    facet_n, pulse_n, order, share, group_len, pulses, bins_dev, k_block,
    after_ref, w_ref, chirp_ref,
):
    mine_f, mine_z = lax.axis_index("facet"), lax.axis_index("pulse")
    k_ids = mine_f * k_block + lax.broadcasted_iota(jnp.int32, (k_block, LANES), 0)
    lane = lax.broadcasted_iota(jnp.int32, (k_block, LANES), 1)
    pulse_dev = pulses // pulse_n

    def rotation(index):
        back = (index + pulses // 2) % pulses - pulses // 2
        cosine, sine = cis_turns(back.astype(f32) * (1.0 / pulses))
        return cosine, -sine

    slot = lane // share
    within = lane % share
    here = (mine_z ^ (slot % pulse_n)) * pulse_dev + (
        within // group_len * facet_n + mine_f
    ) * group_len + within % group_len
    scale = 1.0 / math.sqrt(pulses)
    real, imag = rotation((k_ids * here) % pulses)
    wide = {0: (real * scale, imag * scale)}
    per_block = LANES // share
    turns = []
    bit = 1
    while bit < pulse_n:
        if bit >= per_block:
            sign = 1 - 2 * ((mine_z // bit) % 2)
            turns.append(sign * pulse_dev * bit)
        bit *= 2
    for bit in order:
        sign = 1 - 2 * ((mine_f // bit) % 2)
        turns.append(sign * group_len * bit)
    for level, turn in enumerate(turns):
        rr, ri = rotation((k_ids * turn) % pulses)
        for at in range(1 << level):
            real, imag = wide[at]
            wide[at + (1 << level)] = (real * rr - imag * ri, real * ri + imag * rr)
    for at, (real, imag) in wide.items():
        w_ref[:k_block, at * LANES : at * LANES + LANES] = real.astype(bf16)
        w_ref[k_block:, at * LANES : at * LANES + LANES] = imag.astype(bf16)
    offset = mine_f * k_block - pulses // 2 + lax.broadcasted_iota(jnp.int32, (k_block, bins_dev), 0)
    bins = mine_z * bins_dev + lax.broadcasted_iota(jnp.int32, (k_block, bins_dev), 1)
    phase = (offset * offset).astype(f32) * (8.0 / (2.0 * pulses)) / (8.0 + bins.astype(f32))
    cosine, sine = cis_turns(phase - jnp.round(phase))
    chirp_ref[0] = cosine
    chirp_ref[1] = sine


def transform_tables(after, facet_n, pulse_n, order, share, group_len, pulses, bins_dev, k_block):
    return pl.pallas_call(
        functools.partial(
            transform_tables_kernel, facet_n, pulse_n, order, share, group_len, pulses, bins_dev, k_block
        ),
        out_shape=(
            jax.ShapeDtypeStruct((2 * k_block, pulses), bf16),
            jax.ShapeDtypeStruct((2, k_block, bins_dev), f32),
        ),
        in_specs=[pl.BlockSpec(memory_space=pl.ANY)],
        out_specs=(pl.BlockSpec(memory_space=pltpu.VMEM),) * 2,
        compiler_params=pltpu.CompilerParams(vmem_limit_bytes=16 << 20),
        name="transform_tables",
    )(after)


def transform_kernel(places, has_total, k_block, bins_dev, w_ref, *refs):
    total = refs[0][...] if has_total else None
    pieces = refs[has_total : has_total + len(places)]
    for place, piece in zip(places, pieces):
        rows = piece.shape[0]
        part = jnp.dot(
            w_ref[:, place * rows : place * rows + rows], piece[...], preferred_element_type=f32
        )
        total = part if total is None else total + part
    rest = refs[has_total + len(places) :]
    if len(rest) == 1:
        rest[0][...] = total
        return
    chirp_ref, out_ref = rest
    real = total[:k_block, :bins_dev] - total[k_block:, bins_dev:]
    imag = total[k_block:, :bins_dev] + total[:k_block, bins_dev:]
    cosine, sine = chirp_ref[0], chirp_ref[1]
    out_ref[0] = (cosine * real - sine * imag).T
    out_ref[1] = (cosine * imag + sine * real).T


def transform(w, total, pieces, places, k_block, bins_dev, chirp=None):
    operands = [w] + ([] if total is None else [total]) + [pieces[at] for at in places]
    shape = (2 * k_block, 2 * bins_dev)
    if chirp is not None:
        operands.append(chirp)
        shape = (2, bins_dev, k_block)
    vmem = pl.BlockSpec(memory_space=pltpu.VMEM)
    return pl.pallas_call(
        functools.partial(transform_kernel, places, total is not None, k_block, bins_dev),
        out_shape=jax.ShapeDtypeStruct(shape, f32),
        in_specs=[vmem] * len(operands),
        out_specs=vmem,
        compiler_params=pltpu.CompilerParams(vmem_limit_bytes=16 << 20),
        name="transform",
    )(*operands)


def swap(x, axis, size, mask):
    return lax.ppermute(x, axis, [(i, i ^ mask) for i in range(size)])


def gather_facet(x, size):
    near = [x]
    for mask in range(2, size, 2):
        near.append(swap(x, "facet", size, mask))
    out = []
    for mask, piece in zip(range(0, size, 2), near):
        out += [piece, swap(piece, "facet", size, 1)]
    return out


def body(facet_positions, reflectivity, block_building, visible, platform):
    facet_n = lax.axis_size("facet")
    pulse_n = lax.axis_size("pulse")
    mine_z = lax.axis_index("pulse")
    pulse_dev = platform.shape[1]
    pulses = pulse_dev * pulse_n
    blocks = facet_positions.shape[1] // BLK
    share = pulse_dev // facet_n
    group_len = min(8, share)
    groups = share // group_len
    bins_dev = BINS // pulse_n
    k_block = pulses // facet_n
    buildings = visible.shape[0]

    packed, stations = pack_facets(
        block_building, facet_positions, reflectivity, visible, platform, groups, group_len
    )
    facets = gather_facet(packed, facet_n)

    one = (lax.axis_index("facet") >= 0).astype(bf16)
    fold = jnp.broadcast_to(jnp.asarray(fold_matrix(), bf16)[:, None, :], (256, 8, 256)) * one
    fold = fold.reshape(2048, 256)
    echo = echoes(buildings, stations, fold, facets, blocks, groups, group_len)
    order = [1 << i for i in range(facet_n.bit_length() - 1)]
    w, chirp = transform_tables(
        echo, facet_n, pulse_n, order, share, group_len, pulses, bins_dev, k_block
    )

    echo = echo.reshape(QUADS, groups, 8, 2, LANES)[:, :, :group_len]
    if pulse_n > QUADS:
        echo = echo.reshape(QUADS, share, 2, pulse_n // QUADS, bins_dev).transpose(0, 3, 1, 2, 4)
    echo = echo.reshape(pulse_n, share, 2 * bins_dev)
    turned = [lax.dynamic_index_in_dim(echo, mine_z, 0, keepdims=False)]
    for mask in range(1, pulse_n):
        piece = lax.dynamic_index_in_dim(echo, mine_z ^ mask, 0, keepdims=False)
        turned.append(swap(piece, "pulse", pulse_n, mask))
    turned, w, chirp = lax.optimization_barrier((jnp.concatenate(turned), w, chirp))

    pieces = gather_facet(turned, facet_n)
    total = transform(w, None, pieces, [0, 1], k_block, bins_dev)
    total = transform(w, total, pieces, list(range(2, facet_n, 2)), k_block, bins_dev)
    return transform(w, total, pieces, list(range(3, facet_n, 2)), k_block, bins_dev, chirp)


def solution(mesh):
    placed = (P(None, "facet"), P(None, "facet"), P("facet"), P(None, "pulse"), P(None, "pulse"))
    return jax.shard_map(body, mesh=mesh, in_specs=placed, out_specs=P(None, "pulse", "facet"), check_vma=False)
```

```python
import functools
import math

import jax
import jax.numpy as jnp
import numpy as np
from jax import lax
from jax.experimental import pallas as pl
from jax.experimental.pallas import tpu as pltpu
from jax.sharding import PartitionSpec as P


BLK = 128
PBS = 32
BINS = 512
LANES = 128
WIDE = 8
NARROW = 4
QUADS = 4


f32 = jnp.float32
bf16 = jnp.bfloat16

SIN_C = (4.442882878126042, -7.308239958462742, 3.606233657443361, -0.8453187380162854, 0.10822102663962477)
COS_C = (-1.4142135611352313, 6.978863916510845, -5.739875235214542, 1.8882041596407644, -0.33193097868538995, 0.03399741622323665)


def poly(coefs, w):
    acc = w * coefs[-1] + coefs[-2]
    for c in coefs[-3::-1]:
        acc = acc * w + c
    return acc


def cis_turns(v):
    w = v * v
    s = v * poly(SIN_C, w)
    c = poly(COS_C, w)
    return 1.0 - s * s, -(s * c)


def fold_matrix():
    left = np.zeros((8, 2, 4))
    for m in range(2):
        plus, minus = (2 + m, 1 - m)
        for which, (c, sign) in enumerate(((0, 1), (0, 1), (1, 1), (1, -1))):
            left[m * 4 + which, c, plus] = sign
            left[m * 4 + which, c, minus] = (sign, -sign)[which % 2]
    right = np.zeros((16, 2, 2, 16))
    for f16, ff, m, fn in np.ndindex(2, 2, 2, 2):
        for low in range(2):
            for e, d in ((1, 1), (1, -1), (-1, 1), (-1, -1)):
                far, near = (4, 12)[low], (1, 3)[m]
                sines = f16 + ff + fn
                value = (e if ff else 1) * (d if fn else 1) * (-1) ** (sines // 2)
                right[f16 * 8 + ff * 4 + m * 2 + fn, low, sines % 2, (15 + e * far + d * near) // 2] = value
    both = np.einsum("tca,ulsj->tulcsaj", left, right)
    out = np.zeros((8, 16, 2, 2, 4, 32))
    up, down = slice(16, 32), slice(15, None, -1)
    out[:, :, :, 0, :, up] = both[:, :, :, 0, 0] + both[:, :, :, 1, 1]
    out[:, :, :, 0, :, down] = both[:, :, :, 0, 0] - both[:, :, :, 1, 1]
    out[:, :, :, 1, :, up] = both[:, :, :, 1, 0] - both[:, :, :, 0, 1]
    out[:, :, :, 1, :, down] = both[:, :, :, 1, 0] + both[:, :, :, 0, 1]
    return out.reshape(8 * 32, 2 * 4 * 32) / 32.0


def piece_rows(blocks):
    return -(-(5 * blocks + 2) // 8) * 8


def pack(low, high):
    return jnp.concatenate([low, high], axis=0).astype(bf16)


def block_angles(x, y, z, ax, ay, az):
    dx, dy, dz = x - ax, y - ay, z - az
    d2 = dx * dx + dy * dy + dz * dz
    t = d2 * lax.rsqrt(d2) - 1.25
    w = t * t
    s = t * poly(SIN_C, w)
    return s * poly(COS_C, w), 1.0 - s * s


def block_factors(c1, s1, r0, r1):
    square = c1 * c1
    a2, b2 = 4.0 * square - 2.0, 4.0 * (c1 * s1)
    c3, s3 = (a2 - 1.0) * c1, (a2 + 1.0) * s1
    a4, b4 = a2 * a2 - 2.0, a2 * b2
    a8, b8 = a4 * a4 - 2.0, a4 * b4
    a12, b12 = (a8 - 1.0) * a4, (a8 + 1.0) * b4
    a16, b16 = a8 * a8 - 2.0, a8 * b8
    a32, b32 = a16 * a16 - 2.0, a16 * b16
    a64, b64 = a32 * a32 - 2.0, a32 * b32
    a128, b128 = a64 * a64 - 2.0, a64 * b64
    a256, b256 = a128 * a128 - 2.0, a128 * b128
    a96, b96 = (a64 - 1.0) * a32, (a64 + 1.0) * b32
    c256, s256 = 0.5 * a256, 0.5 * b256
    c144, s144 = a128 * a16 - b128 * b16, b128 * a16 + a128 * b16
    c143, s143 = c144 * c1 + s144 * s1, s144 * c1 - c144 * s1
    q0r, q0i = r0 * c143 + r1 * s143, r1 * c143 - r0 * s143
    q1r, q1i = q0r * c256 + q0i * s256, q0i * c256 - q0r * s256
    q2r, q2i = a256 * q1r - q0r, a256 * q1i - q0i
    q3r, q3i = a256 * q2r - q1r, a256 * q2i - q1i
    return (
        a32, b32, a96, b96, q0r, q0i, q1r, q1i, q2r, q2i, q3r, q3i,
        a16, b16, a4, b4, a12, b12, c1, s1, c3, s3,
    )


def left_table(factors):
    near = [pack(value, value) for value in factors[:4]]
    far = factors[4:]
    tiles = []
    for low in (0, 4):
        real, imag = pack(far[low], far[low + 2]), pack(far[low + 1], far[low + 3])
        for cosine, sine in (near[0:2], near[2:4]):
            tiles += [real * cosine, imag * sine, imag * cosine, real * sine]
    return jnp.concatenate(tiles, axis=0)


def right_table(factors):
    middle = [pack(value, value) for value in factors[:2]]
    far = [pack(factors[2], factors[4]), pack(factors[3], factors[5])]
    near = [pack(value, value) for value in factors[6:]]
    return jnp.concatenate([(m * f) * n for m in middle for f in far for n in near], axis=0)


def echo_kernel(
    pieces, blocks, groups, group_len, buildings,
    platform_ref, fold, *refs,
):
    piece_refs = refs[:pieces]
    out_ref, fac_ref, marks_v, marks_s, rows_s, antenna, angles, products, sem = refs[pieces:]
    mine = lax.axis_index("facet")
    in_turns = 1.0 / (16.0 * math.pi)
    rows = piece_rows(blocks)
    scale = jnp.where(
        lax.broadcasted_iota(jnp.int32, (rows, LANES), 0) < 3 * blocks, in_turns, 1.0
    )
    for piece, ref in enumerate(piece_refs):
        fac_ref[piece * rows : piece * rows + rows, :] = ref[...] * scale
    fac_ref[pieces * rows :, :] = jnp.zeros((rows, LANES), f32)
    ids = jnp.concatenate([ref[5 * blocks : 5 * blocks + 1, :] for ref in piece_refs], axis=0)
    marks = jnp.zeros(ids.shape, jnp.int32)
    for b in range(buildings):
        marks = jnp.where(ids == float(b), piece_refs[0][5 * blocks + 1 : 5 * blocks + 2, b : b + 1].astype(jnp.int32), marks)
    marks_v[:pieces, :] = marks
    marks_v[pieces:, :] = jnp.zeros((8, LANES), jnp.int32)
    marks_copy = pltpu.make_async_copy(marks_v, marks_s, sem)
    marks_copy.start()
    pulse_dev = platform_ref.shape[1]
    flat = platform_ref[...] * in_turns
    flat = jnp.concatenate([flat, jnp.zeros((8 - flat.shape[0], pulse_dev), f32)], axis=0)
    antenna[:pulse_dev, :8] = flat.T
    antenna[pulse_dev:, :] = jnp.zeros((8, LANES), f32)
    marks_copy.wait()
    most = pieces * blocks + 2 * WIDE

    def scan(piece, g, at):
        for j in range(blocks):
            rows_s[at] = piece * rows + j
            at = at + (lax.shift_right_logical(marks_s[piece, j], g) & 1)
        return at

    def close(at):
        for extra in range(2 * WIDE):
            rows_s[at + extra] = pieces * rows

    def station(g):
        g = jnp.minimum(g, groups - 1)
        ant = antenna[pl.ds((g * pieces + mine) * group_len, 8), :]
        return [jnp.broadcast_to(ant[:, i : i + 1], (8, LANES)) for i in range(3)]

    def turn(at, place):
        for j in range(WIDE):
            row = rows_s[at + j]
            facet = [fac_ref[pl.ds(row + blocks * c, 8, stride=0), :] for c in range(3)]
            angles[j, 0], angles[j, 1] = block_angles(*facet, *place)

    def read(at, slot, j):
        row = rows_s[at + j]
        weights = [fac_ref[pl.ds(row + blocks * c, 8, stride=0), :] for c in (3, 4)]
        return angles[slot + j, 0], angles[slot + j, 1], *weights

    same = (
        lax.broadcasted_iota(jnp.int32, (16, 256), 0) % 8
        == lax.broadcasted_iota(jnp.int32, (16, 256), 1) % 8
    )

    def group(acc0, acc1, g, count):
        place = station(g)
        here, there = (g % 2) * most, ((g + 1) % 2) * most
        wide = lax.div(count, WIDE)
        narrow = lax.div(count - wide * WIDE + (NARROW - 1), NARROW)
        narrow = jnp.maximum(narrow, 1 - wide)

        def multiply(at, slot, blocks_here):
            for half in range(blocks_here // 2):
                pair = [block_factors(*read(at, slot, 2 * half + j)) for j in range(2)]
                right = jnp.concatenate([right_table(p[12:]) for p in pair], axis=1)
                left = jnp.concatenate([left_table(p[:12]) for p in pair], axis=1)
                unit, register = half % 2, half // 2
                pltpu.matmul_push_rhs(right, staging_register=register, mxu_index=unit, transpose=True)
                pltpu.matmul_acc_lhs((acc0, acc1)[unit], left, load_staged_rhs=register)

        def wide_step(i, at):
            multiply(here + i * WIDE, 0, WIDE)
            turn(here + (i + 1) * WIDE, place)
            at = scan(jnp.minimum(2 * i, pieces), g + 1, at)
            return scan(jnp.minimum(2 * i + 1, pieces), g + 1, at)

        def narrow_step(i, at):
            multiply(here + wide * WIDE + i * NARROW, i * NARROW, NARROW)
            return scan(jnp.minimum(2 * wide + i, pieces), g + 1, at)

        at = lax.fori_loop(0, wide, wide_step, there)
        at = lax.fori_loop(0, narrow, narrow_step, at)
        at = lax.fori_loop(
            jnp.minimum(2 * wide + narrow, pieces), pieces, lambda piece, n: scan(piece, g + 1, n), at
        )
        close(at)
        turn(there, station(g + 1))
        total = pltpu.matmul_pop(acc0) + pltpu.matmul_pop(acc1)
        for tile in range(16):
            hp, spot = tile // 8, tile % 8
            kept = jnp.where(same, total[tile * 16 : tile * 16 + 16, :], 0.0).astype(bf16)
            products[hp, pl.ds(pl.multiple_of(g * 16, 16), 16), spot * 256 : spot * 256 + 256] = kept
        return at - there

    first = lax.fori_loop(0, pieces, lambda piece, n: scan(piece, 0, n), jnp.int32(0))
    close(first)
    turn(0, station(0))
    pl.run_scoped(
        lambda acc0, acc1: lax.fori_loop(0, groups, functools.partial(group, acc0, acc1), first),
        pltpu.ACC(0)((256, 256), f32), pltpu.ACC(1)((256, 256), f32),
    )
    pl.run_scoped(
        functools.partial(fold_products, groups, products, fold, out_ref),
        pltpu.ACC(0)((groups * 16, 256), f32), pltpu.ACC(1)((groups * 16, 256), f32),
    )


def fold_products(groups, products, fold, out_ref, *accs):
    for k in range(8):
        lanes = slice(k * 256, k * 256 + 256)
        for hp, acc in enumerate(accs):
            pltpu.matmul_push_rhs(fold[lanes, :], staging_register=k % 2, mxu_index=hp)
            pltpu.matmul_acc_lhs(acc, products[hp, :, lanes], load_staged_rhs=k % 2)
    for hp, acc in enumerate(accs):
        echo = pltpu.matmul_pop(acc)
        for low in range(2):
            picked = [echo[g * 16 + low * 8 : g * 16 + low * 8 + 8] for g in range(groups)]
            out_ref[2 * hp + low] = jnp.concatenate(picked, axis=0).astype(bf16)


def echoes(buildings, platform, fold, facets, blocks, groups, group_len):
    pieces = len(facets)
    most = pieces * blocks + 2 * WIDE
    pulse_dev = platform.shape[1]
    vmem = pl.BlockSpec(memory_space=pltpu.VMEM)
    return pl.pallas_call(
        functools.partial(echo_kernel, pieces, blocks, groups, group_len, buildings),
        out_shape=jax.ShapeDtypeStruct((QUADS, groups * 8, 256), bf16),
        in_specs=[vmem] * (2 + pieces),
        out_specs=vmem,
        scratch_shapes=[
            pltpu.VMEM(((pieces + 1) * piece_rows(blocks), LANES), f32),
            pltpu.VMEM((pieces + 8, LANES), jnp.int32),
            pltpu.SMEM((pieces + 8, LANES), jnp.int32),
            pltpu.SMEM((2 * most + 2 * WIDE,), jnp.int32),
            pltpu.VMEM((pulse_dev + 8, LANES), f32),
            pltpu.VMEM((WIDE, 2, 8, LANES), f32),
            pltpu.VMEM((2, groups * 16, 2048), bf16),
            pltpu.SemaphoreType.DMA,
        ],
        compiler_params=pltpu.CompilerParams(vmem_limit_bytes=16 << 20),
        name="echoes",
    )(platform, fold, *facets)


def pack_kernel(
    groups, group_len, ids_hbm, positions_hbm, reflectivity_hbm, visible_hbm, platform_hbm,
    out_ref, stations_ref, ids, positions, reflectivity, visible, sems,
):
    mine, count = lax.axis_index("facet"), lax.axis_size("facet")
    copies = [
        pltpu.make_async_copy(source, target, sems.at[i])
        for i, (source, target) in enumerate((
            (visible_hbm, visible), (ids_hbm, ids),
            (positions_hbm, positions), (reflectivity_hbm, reflectivity), (platform_hbm, stations_ref),
        ))
    ]
    for copy in copies:
        copy.start()
    for copy in copies[:2]:
        copy.wait()
    lane = lax.broadcasted_iota(jnp.int32, (1, LANES), 1)
    row = jnp.zeros(lane.shape, f32)
    for j in range(ids.shape[0]):
        row = jnp.where(lane == j, ids[j].astype(f32), row)
    words = jnp.zeros(lane.shape, jnp.int32)
    columns = [lax.div((g * count + mine) * group_len, PBS) for g in range(groups)]
    for b in range(visible.shape[0]):
        word = jnp.int32(0)
        for g, column in enumerate(columns):
            word = word | lax.shift_left(visible[b, column], g)
        words = jnp.where(lane == b, word, words)
    for copy in copies[2:]:
        copy.wait()
    blocks = ids.shape[0]
    for j in range(blocks):
        lanes = slice(j * LANES, j * LANES + LANES)
        for c in range(3):
            out_ref[c * blocks + j : c * blocks + j + 1, :] = positions[c : c + 1, lanes]
        for c in range(2):
            at = (3 + c) * blocks + j
            out_ref[at : at + 1, :] = reflectivity[c : c + 1, lanes]
    left = out_ref.shape[0] - 5 * blocks
    last = [row, words.astype(f32)] + [jnp.zeros_like(row)] * (left - 2)
    out_ref[5 * blocks :, :] = jnp.concatenate(last, axis=0)


def in_hbm(x):
    return pltpu.with_memory_space_constraint(x, pltpu.HBM)


def pack_facets(ids, positions, reflectivity, visible, platform, groups, group_len):
    vmem = pl.BlockSpec(memory_space=pltpu.VMEM)
    return pl.pallas_call(
        functools.partial(pack_kernel, groups, group_len),
        out_shape=(
            jax.ShapeDtypeStruct((piece_rows(ids.shape[0]), LANES), f32),
            jax.ShapeDtypeStruct(platform.shape, f32),
        ),
        in_specs=[pl.BlockSpec(memory_space=pltpu.HBM)] * 5,
        out_specs=(vmem, vmem),
        scratch_shapes=[
            pltpu.SMEM(ids.shape, jnp.int32),
            pltpu.VMEM(positions.shape, f32),
            pltpu.VMEM(reflectivity.shape, f32),
            pltpu.SMEM(visible.shape, jnp.int32),
            pltpu.SemaphoreType.DMA((5,)),
        ],
        compiler_params=pltpu.CompilerParams(vmem_limit_bytes=4 << 20),
        name="pack_facets",
    )(*map(in_hbm, (ids, positions, reflectivity, visible, platform)))


def transform_tables_kernel(
    facet_n, pulse_n, order, share, group_len, pulses, k_block, after_ref, w_ref,
):
    mine_f, mine_z = lax.axis_index("facet"), lax.axis_index("pulse")
    k_ids = mine_f * k_block + lax.broadcasted_iota(jnp.int32, (k_block, LANES), 0)
    lane = lax.broadcasted_iota(jnp.int32, (k_block, LANES), 1)
    pulse_dev = pulses // pulse_n

    def rotation(index):
        back = (index + pulses // 2) % pulses - pulses // 2
        cosine, sine = cis_turns(back.astype(f32) * (1.0 / pulses))
        return cosine, -sine

    slot = lane // share
    within = lane % share
    here = (mine_z ^ (slot % pulse_n)) * pulse_dev + (
        within // group_len * facet_n + mine_f
    ) * group_len + within % group_len
    scale = 1.0 / math.sqrt(pulses)
    real, imag = rotation((k_ids * here) % pulses)
    wide = {0: (real * scale, imag * scale)}
    per_block = LANES // share
    turns = []
    bit = 1
    while bit < pulse_n:
        if bit >= per_block:
            sign = 1 - 2 * ((mine_z // bit) % 2)
            turns.append(sign * pulse_dev * bit)
        bit *= 2
    for bit in order:
        sign = 1 - 2 * ((mine_f // bit) % 2)
        turns.append(sign * group_len * bit)
    for level, turn in enumerate(turns):
        rr, ri = rotation((k_ids * turn) % pulses)
        for at in range(1 << level):
            real, imag = wide[at]
            wide[at + (1 << level)] = (real * rr - imag * ri, real * ri + imag * rr)
    for at, (real, imag) in wide.items():
        w_ref[:k_block, at * LANES : at * LANES + LANES] = real.astype(bf16)
        w_ref[k_block:, at * LANES : at * LANES + LANES] = imag.astype(bf16)


def chirp_kernel(pulses, bins_dev, k_block, after_ref, chirp_ref):
    mine_f, mine_z = lax.axis_index("facet"), lax.axis_index("pulse")
    offset = mine_f * k_block - pulses // 2 + lax.broadcasted_iota(jnp.int32, (k_block, bins_dev), 0)
    bins = mine_z * bins_dev + lax.broadcasted_iota(jnp.int32, (k_block, bins_dev), 1)
    phase = (offset * offset).astype(f32) * (8.0 / (2.0 * pulses)) / (8.0 + bins.astype(f32))
    cosine, sine = cis_turns(phase - jnp.round(phase))
    chirp_ref[0] = cosine
    chirp_ref[1] = sine


def transform_tables(after, *sizes):
    pulses, k_block = sizes[-2:]
    return pl.pallas_call(
        functools.partial(transform_tables_kernel, *sizes),
        out_shape=jax.ShapeDtypeStruct((2 * k_block, pulses), bf16),
        in_specs=[pl.BlockSpec(memory_space=pl.ANY)],
        out_specs=pl.BlockSpec(memory_space=pltpu.VMEM),
        compiler_params=pltpu.CompilerParams(vmem_limit_bytes=16 << 20),
        name="transform_tables",
    )(after)


def chirp_table(after, pulses, bins_dev, k_block):
    return pl.pallas_call(
        functools.partial(chirp_kernel, pulses, bins_dev, k_block),
        out_shape=jax.ShapeDtypeStruct((2, k_block, bins_dev), f32),
        in_specs=[pl.BlockSpec(memory_space=pl.ANY)],
        out_specs=pl.BlockSpec(memory_space=pltpu.VMEM),
        compiler_params=pltpu.CompilerParams(vmem_limit_bytes=16 << 20),
        name="chirp_table",
    )(after)


def transform_kernel(places, has_total, k_block, bins_dev, w_ref, *refs):
    total = refs[0][...] if has_total else None
    end = has_total + 2 * len(places)
    for i, place in enumerate(places):
        at = has_total + 2 * i
        piece = jnp.concatenate([refs[at][...], refs[at + 1][...]], axis=0)
        rows = piece.shape[0]
        part = jnp.dot(
            w_ref[:, place * rows : place * rows + rows], piece, preferred_element_type=f32
        )
        total = part if total is None else total + part
    rest = refs[end:]
    if len(rest) == 1:
        rest[0][...] = total
        return
    chirp_ref, out_ref = rest
    real = total[:k_block, :bins_dev] - total[k_block:, bins_dev:]
    imag = total[k_block:, :bins_dev] + total[:k_block, bins_dev:]
    cosine, sine = chirp_ref[0], chirp_ref[1]
    out_ref[0] = (cosine * real - sine * imag).T
    out_ref[1] = (cosine * imag + sine * real).T


def transform(w, total, pieces, places, k_block, bins_dev, chirp=None):
    operands = [w] + ([] if total is None else [total])
    for at in places:
        operands += pieces[at]
    shape = (2 * k_block, 2 * bins_dev)
    if chirp is not None:
        operands.append(chirp)
        shape = (2, bins_dev, k_block)
    vmem = pl.BlockSpec(memory_space=pltpu.VMEM)
    return pl.pallas_call(
        functools.partial(transform_kernel, places, total is not None, k_block, bins_dev),
        out_shape=jax.ShapeDtypeStruct(shape, f32),
        in_specs=[vmem] * len(operands),
        out_specs=vmem,
        compiler_params=pltpu.CompilerParams(vmem_limit_bytes=16 << 20),
        name="transform",
    )(*operands)


def swap(x, axis, size, mask):
    return lax.ppermute(x, axis, [(i, i ^ mask) for i in range(size)])


def gather_facet(x, size):
    near = [x]
    for mask in range(2, size, 2):
        near.append(swap(x, "facet", size, mask))
    out = []
    for mask, piece in zip(range(0, size, 2), near):
        out += [piece, swap(piece, "facet", size, 1)]
    return out


def body(facet_positions, reflectivity, block_building, visible, platform):
    facet_n = lax.axis_size("facet")
    pulse_n = lax.axis_size("pulse")
    mine_z = lax.axis_index("pulse")
    pulse_dev = platform.shape[1]
    pulses = pulse_dev * pulse_n
    blocks = facet_positions.shape[1] // BLK
    share = pulse_dev // facet_n
    group_len = min(8, share)
    groups = share // group_len
    bins_dev = BINS // pulse_n
    k_block = pulses // facet_n
    buildings = visible.shape[0]

    packed, stations = pack_facets(
        block_building, facet_positions, reflectivity, visible, platform, groups, group_len
    )
    facets = gather_facet(packed, facet_n)

    one = (lax.axis_index("facet") >= 0).astype(bf16)
    fold = jnp.broadcast_to(jnp.asarray(fold_matrix(), bf16)[:, None, :], (256, 8, 256)) * one
    fold = fold.reshape(2048, 256)
    echo = echoes(buildings, stations, fold, facets, blocks, groups, group_len)
    order = [1 << i for i in range(facet_n.bit_length() - 1)]
    w = transform_tables(echo, facet_n, pulse_n, order, share, group_len, pulses, k_block)
    chirp = chirp_table(echo, pulses, bins_dev, k_block)

    echo = echo.reshape(QUADS, groups, 8, 2, LANES)[:, :, :group_len]
    if pulse_n > QUADS:
        echo = echo.reshape(QUADS, share, 2, pulse_n // QUADS, bins_dev).transpose(0, 3, 1, 2, 4)
    echo = echo.reshape(pulse_n, share, 2 * bins_dev)
    turned = [lax.dynamic_index_in_dim(echo, mine_z, 0, keepdims=False)]
    for mask in range(1, pulse_n):
        piece = lax.dynamic_index_in_dim(echo, mine_z ^ mask, 0, keepdims=False)
        turned.append(swap(piece, "pulse", pulse_n, mask))

    first = gather_facet(turned[0], facet_n)
    rest = gather_facet(jnp.concatenate(turned[1:]), facet_n)
    pieces = list(zip(first, rest))
    total = transform(w, None, pieces, [0, 1], k_block, bins_dev)
    total = transform(w, total, pieces, list(range(2, facet_n, 2)), k_block, bins_dev)
    return transform(w, total, pieces, list(range(3, facet_n, 2)), k_block, bins_dev, chirp)


def solution(mesh):
    placed = (P(None, "facet"), P(None, "facet"), P("facet"), P(None, "pulse"), P(None, "pulse"))
    return jax.shard_map(body, mesh=mesh, in_specs=placed, out_specs=P(None, "pulse", "facet"), check_vma=False)
```
